32 devices in a mesh: row: 4 (over x, core), col: 8 (over z, y).
Axes of the slice: x: 2, y: 2, z: 4, core: 2. Of those that a mesh axis runs over, the one named last changes fastest.
Arguments:
- heat_source: bfloat16 [262144, 128], P(('row', 'col')), may hold values from -6 to 6
- diagonal: float32 [262144], P(('row', 'col')), may hold values from 3 to 8
- active: int32 [262144], P(('row', 'col')), may hold values 0 or 1
- conductance: bfloat16 [2048, 7, 128, 128], P(('row', 'col')), may hold values from -0.1875 to 0.1875
- pattern: int32 [2048, 7], P(('row', 'col')), may hold values from 0 to 127, as said below
- send_list: int32 [32, 4, 16], P(('row', 'col')), may hold values from 0 to 63
- owner_map: int32 [2, 2048], replicated, may hold values from 0 to 63, as said below
- displacement: bfloat16 [64, 32, 128, 128], P('row', 'col'), may hold values from -6 to 6
- bond_live: int32 [6, 64, 32, 128], P(None, 'row', 'col'), may hold values from 0 to 1, as said below
Outputs:
- brick_temperature: bfloat16 [64, 32, 128, 128], P('row', 'col')
- moved: bfloat16 [64, 32, 128, 128], P('row', 'col')
The draws below stay inside these ranges and needn't reach their ends.
Inputs may be any that keep to these rules, and one draw needn't show every extreme that they name: `pattern`: tile 0 of a block row reads the block itself (its row within the device); tile 1 reads received slot 64 + that row. `owner_map`: every brick slot receives exactly one block. Brick slot s is fed from the device a fixed cyclic distance back along the curve order, the same distance for every brick; one device sends exactly 2 blocks to some bricks and at most that to any. bond_live[d + 3] at a cell equals bond_live[d] at the cell one step back along direction d, and 0 where that cell lies outside the grid; bonds leaving the grid in + directions are 0. `send_list`: local block indices.
All inputs are finite; a program needn't handle non-finite values. No bound on the sum of `active` on one device may be relied on, other than what follows from the above.
Results may differ from the reference program's by a relative error of at most 0.004.
Values may be sent and summed in bfloat16 or wider, within the bound.
A program may use at most 192 MiB of HBM per device.

```python
import math
import jax
import jax.numpy as jnp
from jax import lax

BX = 16
BY = 4
NODES_PER_COLUMN = 128
PROCESS_CASES = 128
TILES = 7
ITERS = 3
BLK_DEV = 64
GHOST_CAP = 16
PATH_SEGMENTS = 2048
POINTS = 262144
X = 64
Y = 32
N_ROW = 4
N_COL = 8
DEVICES = 32


def draw_pattern(key, part):
    rows_local = jnp.arange(PATH_SEGMENTS, dtype=jnp.int32) % BLK_DEV
    others = jax.random.randint(key, (PATH_SEGMENTS, TILES - 2), 0, 2 * BLK_DEV, dtype=jnp.int32)
    return jnp.concatenate([rows_local[:, None], (rows_local + BLK_DEV)[:, None], others], 1).astype(jnp.int32)


def draw_owner_map(key, part):
    first_key, second_key = jax.random.split(jax.random.fold_in(key, 11))
    span = max(DEVICES, BLK_DEV)
    scores = jax.random.permutation(first_key, span).astype(jnp.int32)
    values = jnp.arange(span, dtype=jnp.int32)
    scores = jnp.where(values == 1, -2, scores)
    scores = jnp.where(values == DEVICES // 2, -1, scores)
    ordered = jnp.argsort(scores, stable=True).astype(jnp.int32)
    offsets = ordered[:BLK_DEV] % DEVICES
    slots = jax.vmap(lambda subkey: jax.random.permutation(subkey, BLK_DEV))(jax.random.split(second_key, DEVICES))
    sources = jnp.arange(DEVICES, dtype=jnp.int32)[:, None]
    targets = (sources + offsets[slots]) % DEVICES
    return jnp.stack([targets.reshape(-1), slots.reshape(-1)]).astype(jnp.int32)


def draw_bond_live(key, part):
    raw = jax.random.randint(key, (3, X, Y, NODES_PER_COLUMN), 0, 8, dtype=jnp.int32)
    live = (raw < 7).astype(jnp.int32)
    plus_x = live[0].at[-1].set(0)
    plus_y = live[1].at[:, -1].set(0)
    plus_z = live[2].at[:, :, -1].set(0)
    minus_x = jnp.concatenate([jnp.zeros_like(plus_x[:1]), plus_x[:-1]], 0)
    minus_y = jnp.concatenate([jnp.zeros_like(plus_y[:, :1]), plus_y[:, :-1]], 1)
    minus_z = jnp.concatenate([jnp.zeros_like(plus_z[:, :, :1]), plus_z[:, :, :-1]], 2)
    return jnp.stack([plus_x, plus_y, plus_z, minus_x, minus_y, minus_z]).astype(jnp.int32)


def touch_ends(drawn, stream_key, smallest, high):
    longest = drawn.shape.index(max(drawn.shape))
    spots = []
    for shift in (0, 1):
        where = [jax.random.randint(jax.random.fold_in(stream_key, axis), (), 0, length) for axis, length in enumerate(drawn.shape)]
        where[longest] = (where[longest] + shift) % drawn.shape[longest]
        spots.append(tuple(where))
    return drawn.at[spots[0]].set(smallest).at[spots[1]].set(high)


def levels(stream_key, dims, cuts, smallest, high):
    gain = 1.0
    for dim, shards_of in cuts:
        draws = jax.random.uniform(jax.random.fold_in(jax.random.fold_in(stream_key, 6), dim), (shards_of,), jnp.float32, smallest / len(cuts), high / len(cuts))
        gain = gain * jnp.repeat(jnp.exp(draws), dims[dim] // shards_of).reshape((-1,) + (1,) * (len(dims) - 1 - dim))
    return gain


def gaussian(key, extent, deviation, most, cuts=(), held_as=jnp.bfloat16):
    drawn = deviation * jax.random.normal(key, extent, jnp.float32)
    if cuts:
        drawn = drawn * levels(key, extent, cuts, -0.22, 0.18)
    return jnp.clip(drawn, -most, most).astype(held_as)


def setup_inputs(seed: int = 0) -> dict:
    splits = jax.random.split(jax.random.key(seed), 10)
    return {
        "heat_source": gaussian(splits[0], (POINTS, PROCESS_CASES), 1.0, 6.0, ((0, 32),)),
        "diagonal": jnp.clip(jnp.exp(math.log(8.0) - 0.98082925 * jax.random.uniform(splits[1], (POINTS,), jnp.float32) ** levels(splits[1], (POINTS,), ((0, 32),), -0.2, 0.2)), 3.0, 8.0),
        "active": touch_ends((jax.random.randint(splits[2], (POINTS,), 0, 4) < 3).astype(jnp.int32), jax.random.fold_in(splits[2], 1), 0, 1),
        "conductance": gaussian(splits[3], (PATH_SEGMENTS, TILES, NODES_PER_COLUMN, NODES_PER_COLUMN), (TILES * NODES_PER_COLUMN) ** -0.5, 0.1875, ((0, 32),)),
        "pattern": draw_pattern(jax.random.fold_in(splits[9], 71), 0),
        "send_list": touch_ends(jax.random.randint(splits[5], (DEVICES, 4, GHOST_CAP), 0, BX * BY), jax.random.fold_in(splits[5], 1), 0, (BX * BY) - 1).astype(jnp.int32),
        "owner_map": draw_owner_map(jax.random.fold_in(splits[9], 71), 0),
        "displacement": gaussian(splits[7], (X, Y, NODES_PER_COLUMN, PROCESS_CASES), 1.0, 6.0, ((0, 4), (1, 8))),
        "bond_live": draw_bond_live(jax.random.fold_in(splits[9], 71), 0),
    }


LOWER = 1.0
UPPER = 10.0
ALPHA_T = 0.5
BOND_STIFFNESS = 1.0
STATE_STIFFNESS = 2.0
STEP_SIZE = 0.1
GHOST_STEPS = (1, -1, 2, -2)


def chebyshev_weights(count):
    center = (UPPER + LOWER) / 2.0
    half_width = (UPPER - LOWER) / 2.0
    ratio_value = center / half_width
    previous = 1.0 / ratio_value
    weights = []
    for step_number in range(count):
        current = 1.0 / (2.0 * ratio_value - previous)
        weights.append((current * previous, 2.0 * current / half_width))
        previous = current
    return 1.0 / center, weights


def global_columns(pattern, send_list):
    blocks = pattern.shape[0]
    devices = send_list.shape[0]
    per_device = blocks // devices
    ghost_cap = send_list.shape[2]
    owner_dev = jnp.arange(blocks, dtype=jnp.int32) // per_device
    is_local = pattern < per_device
    ghost_slot = jnp.maximum(pattern - per_device, 0)
    group_num = ghost_slot // ghost_cap
    within = ghost_slot % ghost_cap
    step_table = jnp.array(GHOST_STEPS, dtype=jnp.int32)
    source = owner_dev[:, None] - step_table[group_num]
    valid = (source >= 0) & (source < devices)
    safe_source = jnp.clip(source, 0, devices - 1)
    sent_block = send_list[safe_source, group_num, within]
    ghost_global = safe_source * per_device + sent_block
    local_global = owner_dev[:, None] * per_device + pattern
    chosen = jnp.where(is_local, local_global, jnp.where(valid, ghost_global, blocks))
    return chosen.astype(jnp.int32)


def apply_operator(pair_unit_vector, diagonal, active_f, conductance, columns):
    blocks = columns.shape[0]
    masked = (pair_unit_vector * active_f[:, None]).astype(jnp.bfloat16)
    padded = jnp.concatenate([masked.reshape(blocks, NODES_PER_COLUMN, PROCESS_CASES), jnp.zeros((1, NODES_PER_COLUMN, PROCESS_CASES), jnp.bfloat16)], 0)
    total = jnp.zeros((blocks, NODES_PER_COLUMN, PROCESS_CASES), jnp.float32)
    for tile_k in range(TILES):
        chosen = padded[columns[:, tile_k]].astype(jnp.float32)
        total = total + jnp.einsum("bij,bjr->bir", conductance[:, tile_k].astype(jnp.float32), chosen)
    return diagonal[:, None] * pair_unit_vector + active_f[:, None] * total.reshape(-1, PROCESS_CASES)


def neighbour(field, axis_num, sign):
    size = field.shape[axis_num]
    widths = [(0, 0)] * field.ndim
    widths[axis_num] = (1, 1)
    padded = jnp.pad(field, widths)
    return lax.slice_in_dim(padded, 1 + sign, 1 + sign + size, axis=axis_num)


def mechanics(displacement, lattice_nodes, bond_live):
    moving = displacement.astype(jnp.float32)
    heat = lattice_nodes.astype(jnp.float32)
    live = bond_live.astype(jnp.float32)
    directions = [(0, 1), (1, 1), (2, 1), (0, -1), (1, -1), (2, -1)]

    def stretch_of(axis_num, sign):
        return neighbour(moving, axis_num, sign) - moving - ALPHA_T * 0.5 * (heat + neighbour(heat, axis_num, sign))

    volume_dilatation = jnp.zeros_like(moving)
    for bond_count, (axis_num, sign) in enumerate(directions):
        volume_dilatation = volume_dilatation + live[bond_count][..., None] * stretch_of(axis_num, sign)
    volume_dilatation = volume_dilatation / 6.0
    force = jnp.zeros_like(moving)
    for bond_count, (axis_num, sign) in enumerate(directions):
        series_term = BOND_STIFFNESS * stretch_of(axis_num, sign) + STATE_STIFFNESS * (neighbour(volume_dilatation, axis_num, sign) - volume_dilatation)
        force = force + live[bond_count][..., None] * series_term
    return (moving + STEP_SIZE * force).astype(jnp.bfloat16)


def reference(heat_source, diagonal, active, conductance, pattern, send_list, owner_map, displacement, bond_live):
    columns = global_columns(pattern, send_list)
    active_f = active.astype(jnp.float32)
    first_scale, weights = chebyshev_weights(ITERS)
    residual = heat_source.astype(jnp.float32)
    pair_unit_vector = residual * first_scale
    computed_heat_map = jnp.zeros_like(residual)
    for old_weight, res_weight in weights:
        image = apply_operator(pair_unit_vector, diagonal, active_f, conductance, columns)
        computed_heat_map = computed_heat_map + pair_unit_vector
        residual = residual - image
        pair_unit_vector = old_weight * pair_unit_vector + res_weight * residual
    thermal_profile = (computed_heat_map + pair_unit_vector).astype(jnp.bfloat16)
    desired_quantity = (owner_map[0] * BLK_DEV + owner_map[1]).astype(jnp.int32)
    lattice_nodes = jnp.zeros((PATH_SEGMENTS, NODES_PER_COLUMN, PROCESS_CASES), jnp.bfloat16).at[desired_quantity].set(thermal_profile.reshape(PATH_SEGMENTS, NODES_PER_COLUMN, PROCESS_CASES))
    lattice_nodes = lattice_nodes.reshape(N_ROW, N_COL, BX, BY, NODES_PER_COLUMN, PROCESS_CASES).transpose(0, 2, 1, 3, 4, 5).reshape(X, Y, NODES_PER_COLUMN, PROCESS_CASES)
    moved = mechanics(displacement, lattice_nodes, bond_live)
    return lattice_nodes, moved
```

```python
import functools

import jax
import jax.numpy as jnp
from jax import lax
from jax.experimental import pallas as pl
from jax.experimental.pallas import tpu as pltpu
from jax.sharding import PartitionSpec as P

ITERS = 3
LOWER = 1.0
UPPER = 10.0
ALPHA_T = 0.5
BOND_STIFFNESS = 1.0
STATE_STIFFNESS = 2.0
STEP_SIZE = 0.1
GHOST_STEPS = (1, -1, 2, -2)
SEND_ORDER = (2, 3, 0, 1)
HALO_CHUNKS = 4
MESH = pl.DeviceIdType.MESH
MIB = 1024 * 1024


def chebyshev_weights(count):
    center = (UPPER + LOWER) / 2.0
    half_width = (UPPER - LOWER) / 2.0
    ratio_value = center / half_width
    previous = 1.0 / ratio_value
    weights = []
    for step_number in range(count):
        current = 1.0 / (2.0 * ratio_value - previous)
        weights.append((current * previous, 2.0 * current / half_width))
        previous = current
    return (1.0 / center, weights)


def curve_kernel(
    pattern,
    send_list,
    table,
    heat_hbm,
    active,
    diagonal,
    conductance,
    bricks,
    tiles,
    heat,
    ext0,
    ext1,
    ext2,
    outgoing,
    residual,
    direction,
    total,
    active_wide,
    diagonal_wide,
    arrived,
    tile_sem,
    heat_sem,
    send_sem,
    recv_sem,
    out_sem,
    in_sem,
):
    rows, cols = lax.axis_size("row"), lax.axis_size("col")
    devices = rows * cols
    me = lax.axis_index("row") * cols + lax.axis_index("col")
    blocks, length, cases = heat.shape
    tile_count = tiles.shape[1]
    cap = send_list.shape[2]
    ghosts = cap * len(GHOST_STEPS)
    share = arrived.shape[0] // devices
    exts = (ext0, ext1, ext2)
    first_scale, weights = chebyshev_weights(ITERS)

    heat_copy = pltpu.make_async_copy(heat_hbm, heat, heat_sem)
    heat_copy.start()
    tile_copy = pltpu.make_async_copy(conductance, tiles, tile_sem)
    tile_copy.start()

    def inside(index):
        return jnp.logical_and(index >= 0, index < devices)

    def place(index):
        return (lax.div(index, cols), lax.rem(index, cols))

    barrier = pltpu.get_barrier_semaphore()

    @pl.loop(1, devices)
    def _(i):
        peer = lax.rem(me + i, devices)
        pl.semaphore_signal(barrier, inc=1, device_id=place(peer), device_id_type=MESH)

    def ghost_copy(it, group):
        return pltpu.make_async_remote_copy(
            src_ref=outgoing.at[pl.ds((it % 2) * ghosts + group * cap, cap)],
            dst_ref=exts[it].at[pl.ds(blocks + group * cap, cap)],
            send_sem=send_sem.at[it, group],
            recv_sem=recv_sem.at[it, group],
            device_id=place(me + GHOST_STEPS[group]),
            device_id_type=MESH,
        )

    def brick_copy(target, source):
        return pltpu.make_async_remote_copy(
            src_ref=outgoing.at[pl.ds((ITERS % 2) * ghosts + target * share, share)],
            dst_ref=arrived.at[pl.ds(source * share, share)],
            send_sem=out_sem.at[target],
            recv_sem=in_sem.at[source],
            device_id=place(target),
            device_id_type=MESH,
        )

    wide = jnp.concatenate([active[...].astype(jnp.float32), diagonal[...]], axis=0).T
    for b in range(blocks):
        column = jnp.broadcast_to(wide[:, b : b + 1], (length, cases))
        active_wide[b] = column.astype(jnp.bfloat16)

    heat_copy.wait()

    def first_value(b):
        start = heat[b].astype(jnp.float32) * first_scale
        return (start * active_wide[b].astype(jnp.float32)).astype(jnp.bfloat16)

    for group in SEND_ORDER:

        @pl.loop(0, cap)
        def _(j):
            outgoing[group * cap + j] = first_value(send_list[0, group, j])

        if group == SEND_ORDER[0]:
            pl.semaphore_wait(barrier, devices - 1)

        @pl.when(inside(me + GHOST_STEPS[group]))
        def _():
            ghost_copy(0, group).start()

    for it in range(ITERS):
        for group, step in enumerate(GHOST_STEPS):

            @pl.when(jnp.logical_not(inside(me - step)))
            def _():
                exts[it][pl.ds(blocks + group * cap, cap)] = jnp.zeros(
                    (cap, length, cases), jnp.bfloat16
                )

    for b in range(blocks):
        diagonal_wide[b] = jnp.broadcast_to(
            wide[:, blocks + b : blocks + b + 1], (length, cases)
        )

    @pl.loop(0, blocks)
    def _(b):
        source = heat[b].astype(jnp.float32)
        residual[b] = source
        direction[b] = source * first_scale
        ext0[b] = first_value(b)

    tile_copy.wait()

    for it in range(ITERS):
        ext = exts[it]
        old_weight, res_weight = weights[it]
        last = it == ITERS - 1

        @pl.loop(0, blocks)
        def _(b):
            own = jnp.dot(tiles[b, 0], ext[b], preferred_element_type=jnp.float32)
            held = direction[b]
            left = (
                residual[b] - diagonal_wide[b] * held - active_wide[b].astype(jnp.float32) * own
            )
            mixed = old_weight * held + res_weight * left
            summed = held if it == 0 else total[b] + held
            if last:
                total[b] = summed + mixed
            else:
                residual[b] = left
                direction[b] = mixed
                total[b] = summed

        for group, step in enumerate(GHOST_STEPS):

            @pl.when(inside(me - step))
            def _():
                ghost_copy(it, group).wait_recv()

        def far_of(b):
            chosen = [ext[blocks + b]]
            for k in range(2, tile_count):
                chosen.append(ext[pattern[b, k]])
            row = jnp.concatenate([tiles[b, k] for k in range(1, tile_count)], axis=1)
            far = jnp.dot(row, jnp.concatenate(chosen, axis=0), preferred_element_type=jnp.float32)
            return active_wide[b].astype(jnp.float32) * far

        if not last:
            for group in SEND_ORDER:
                if it > 0:

                    @pl.when(inside(me + GHOST_STEPS[group]))
                    def _():
                        ghost_copy(it - 1, group).wait_send()

                @pl.loop(0, cap, unroll=2)
                def _(j):
                    b = send_list[0, group, j]
                    value = direction[b] - res_weight * far_of(b)
                    outgoing[(it + 1) % 2 * ghosts + group * cap + j] = (
                        value * active_wide[b].astype(jnp.float32)
                    ).astype(jnp.bfloat16)

                @pl.when(inside(me + GHOST_STEPS[group]))
                def _():
                    ghost_copy(it + 1, group).start()

            @pl.loop(0, blocks, unroll=2)
            def _(b):
                far = far_of(b)
                residual[b] = residual[b] - far
                held = direction[b] - res_weight * far
                direction[b] = held
                exts[it + 1][b] = (held * active_wide[b].astype(jnp.float32)).astype(jnp.bfloat16)

        else:
            for group, step in enumerate(GHOST_STEPS):

                @pl.when(inside(me + step))
                def _():
                    ghost_copy(it - 1, group).wait_send()

            def final(b):
                return (total[b] - res_weight * far_of(b)).astype(jnp.bfloat16)

            @pl.loop(1, devices)
            def _(i):
                target = lax.rem(me + i, devices)
                for r in range(share):
                    outgoing[ITERS % 2 * ghosts + target * share + r] = final(table[target * share + r])
                brick_copy(target, me).start()

            for r in range(share):
                arrived[me * share + r] = final(table[me * share + r])

    for group, step in enumerate(GHOST_STEPS):

        @pl.when(inside(me + step))
        def _():
            ghost_copy(ITERS - 1, group).wait_send()

    @pl.loop(1, devices)
    def _(i):
        brick_copy(me, lax.rem(me + devices - i, devices)).wait_recv()

    @pl.loop(0, blocks)
    def _(s):
        bricks[s] = arrived[table[devices * share + s]]

    @pl.loop(1, devices)
    def _(i):
        brick_copy(lax.rem(me + i, devices), me).wait_send()


def curve(pattern, send_list, table, heat, active, diagonal, conductance, devices):
    blocks, length, cases = heat.shape
    ghosts = send_list.shape[1] * send_list.shape[2]
    places = table.shape[0] - blocks
    smem = pl.BlockSpec(memory_space=pltpu.SMEM)
    vmem = pl.BlockSpec(memory_space=pltpu.VMEM)
    hbm = pl.BlockSpec(memory_space=pl.ANY)
    state = pltpu.VMEM((blocks, length, cases), jnp.float32)
    ext = pltpu.VMEM((blocks + ghosts, length, cases), jnp.bfloat16)
    half = pltpu.VMEM((blocks, length, cases), jnp.bfloat16)
    dma = pltpu.SemaphoreType.DMA
    return pl.pallas_call(
        curve_kernel,
        out_shape=jax.ShapeDtypeStruct((blocks, length, cases), jnp.bfloat16),
        in_specs=[smem, smem, smem, hbm, vmem, vmem, hbm],
        out_specs=vmem,
        scratch_shapes=[
            pltpu.VMEM(conductance.shape, jnp.bfloat16),
            half,
            ext,
            ext,
            ext,
            pltpu.VMEM((ghosts + max(ghosts, places), length, cases), jnp.bfloat16),
            state,
            state,
            state,
            half,
            state,
            pltpu.VMEM((places, length, cases), jnp.bfloat16),
            dma,
            dma,
            dma((ITERS, len(GHOST_STEPS))),
            dma((ITERS, len(GHOST_STEPS))),
            dma((devices,)),
            dma((devices,)),
        ],
        compiler_params=pltpu.CompilerParams(
            collective_id=0, has_side_effects=True, vmem_limit_bytes=60 * MIB
        ),
        name="curve",
    )(pattern, send_list, table, heat, active, diagonal, conductance)


def mechanics_kernel(
    bricks, displacement, bonds, moved, live, field, dilated, part, sem_y, sem_x
):
    rows, cols = lax.axis_size("row"), lax.axis_size("col")
    row, col = lax.axis_index("row"), lax.axis_index("col")
    nx, ny = displacement.shape[:2]
    length, cases = displacement.shape[2:]
    cells = nx * ny
    chunks = HALO_CHUNKS
    piece = nx // chunks
    scale = ALPHA_T * 0.5

    beside = (
        (col + 1 < cols, (row, col + 1)),
        (col > 0, (row, col - 1)),
        (row + 1 < rows, (row + 1, col)),
        (row > 0, (row - 1, col)),
    )
    behind = (1, 0, 3, 2)

    barrier = pltpu.get_barrier_semaphore()
    peers = 0
    for there, where in beside:
        peers = peers + jnp.where(there, 1, 0)

        @pl.when(there)
        def _():
            pl.semaphore_signal(barrier, inc=1, device_id=where, device_id_type=MESH)

    def copy_y(buffer, turn, way, chunk):
        cut = pl.ds(1 + chunk * piece, piece)
        return pltpu.make_async_remote_copy(
            src_ref=buffer.at[cut, ny if way == 0 else 1],
            dst_ref=buffer.at[cut, 0 if way == 0 else ny + 1],
            send_sem=sem_y.at[turn, 0, way, chunk],
            recv_sem=sem_y.at[turn, 1, way, chunk],
            device_id=beside[way][1],
            device_id_type=MESH,
        )

    def copy_x(buffer, turn, way):
        cut = pl.ds(1, ny)
        return pltpu.make_async_remote_copy(
            src_ref=buffer.at[nx if way == 2 else 1, cut],
            dst_ref=buffer.at[0 if way == 2 else nx + 1, cut],
            send_sem=sem_x.at[turn, 0, way - 2],
            recv_sem=sem_x.at[turn, 1, way - 2],
            device_id=beside[way][1],
            device_id_type=MESH,
        )

    def pair(x, y):
        moving = displacement[x, y].astype(jnp.float32)
        heat = scale * bricks[x, y].astype(jnp.float32)
        return moving, heat

    def store_field(x, y):
        moving, heat = pair(x, y)
        field[x + 1, y + 1] = (moving - heat).astype(jnp.bfloat16)

    for y in (0, ny - 1):

        @pl.loop(0, nx)
        def _(x):
            store_field(x, y)

    for y in range(1, ny - 1):
        store_field(0, y)
        store_field(nx - 1, y)

    pl.semaphore_wait(barrier, peers)
    for way in (2, 3):

        @pl.when(beside[way][0])
        def _():
            copy_x(field, 0, way).start()

    order = (0, chunks - 1, *range(1, chunks - 1))
    for chunk in order:
        for way in (0, 1):

            @pl.when(beside[way][0])
            def _():
                copy_y(field, 0, way, chunk).start()

    for y in range(1, ny - 1):

        @pl.loop(1, nx - 1)
        def _(x):
            store_field(x, y)

    for buffer in (field, dilated):
        for way, at in ((0, 0), (1, ny + 1)):

            @pl.when(jnp.logical_not(beside[behind[way]][0]))
            def _():
                buffer[pl.ds(1, nx), at] = jnp.zeros((nx, length, cases), jnp.bfloat16)

        for way, at in ((2, 0), (3, nx + 1)):

            @pl.when(jnp.logical_not(beside[behind[way]][0]))
            def _():
                buffer[at, pl.ds(1, ny)] = jnp.zeros((ny, length, cases), jnp.bfloat16)

    group = 8
    for half in range(3):
        flags = bonds[pl.ds(half * 2 * cells, 2 * cells)].astype(jnp.float32).T

        for g in range(2 * cells // group):
            for j in range(group):
                at = g * group + j
                live[half * 2 + at // cells, at % cells] = jnp.broadcast_to(
                    flags[:, at : at + 1], (length, cases)
                ).astype(jnp.bfloat16)

    def flag(d, x, y):
        return live[d, x * ny + y].astype(jnp.float32)

    def up(value):
        return pltpu.roll(value, length - 1, 0)

    def down(value):
        return pltpu.roll(value, 1, 0)

    def inner_sum(buffer, centre, x, y, first, final):
        along_up, along_down = flag(2, x, y), flag(5, x, y)
        total = along_up * up(centre) + along_down * down(centre)
        count = along_up + along_down
        for d, dx, dy, within in (
            (0, 1, 0, not final),
            (3, -1, 0, not first),
            (1, 0, 1, y < ny - 1),
            (4, 0, -1, y > 0),
        ):
            bond = flag(d, x, y)
            count = count + bond
            if within:
                total = total + bond * buffer[x + 1 + dx, y + 1 + dy].astype(jnp.float32)
        return total, count

    def every_cell(body):
        for y in range(ny):
            body(0, y, True, False)

            @pl.loop(1, nx - 1)
            def _(x):
                body(x, y, False, False)

            body(nx - 1, y, False, True)

    def stretch_cell(x, y, first, final):
        moving, heat = pair(x, y)
        total, count = inner_sum(field, moving - heat, x, y, first, final)
        value = (total - count * (moving + heat)) * (1.0 / 6.0)
        part[x * ny + y] = value
        if 0 < y < ny - 1 and not first and not final:
            dilated[x + 1, y + 1] = value.astype(jnp.bfloat16)

    every_cell(stretch_cell)

    def edge_x(at, way):
        return (0, 0, 3) if way == 2 else (nx - 1, nx + 1, 0)

    for way in (2, 3):

        @pl.when(beside[behind[way]][0])
        def _():
            copy_x(field, 0, way).wait_recv()

        x, halo, d = edge_x(0, way)
        for y in range(ny):
            value = part[x * ny + y] + flag(d, x, y) * field[halo, y + 1].astype(jnp.float32) * (
                1.0 / 6.0
            )
            part[x * ny + y] = value
            if 0 < y < ny - 1:
                dilated[x + 1, y + 1] = value.astype(jnp.bfloat16)

    for chunk in order:
        for way, y, halo, d in ((0, 0, 0, 4), (1, ny - 1, ny + 1, 1)):

            @pl.when(beside[behind[way]][0])
            def _():
                copy_y(field, 0, way, chunk).wait_recv()

            for i in range(piece):
                x = chunk * piece + i
                value = part[x * ny + y] + flag(d, x, y) * field[x + 1, halo].astype(
                    jnp.float32
                ) * (1.0 / 6.0)
                part[x * ny + y] = value
                dilated[x + 1, y + 1] = value.astype(jnp.bfloat16)

            out = behind[way]

            @pl.when(beside[out][0])
            def _():
                copy_y(dilated, 1, out, chunk).start()

        if chunk == 0:

            @pl.when(beside[3][0])
            def _():
                copy_x(dilated, 1, 3).start()

        if chunk == chunks - 1:

            @pl.when(beside[2][0])
            def _():
                copy_x(dilated, 1, 2).start()

    def force_cell(x, y, first, final):
        moving = displacement[x, y].astype(jnp.float32)
        centre = part[x * ny + y]
        total, count = inner_sum(dilated, centre, x, y, first, final)
        force = BOND_STIFFNESS * 6.0 * centre + STATE_STIFFNESS * (total - count * centre)
        value = moving + STEP_SIZE * force
        if 0 < y < ny - 1 and not first and not final:
            moved[x, y] = value.astype(jnp.bfloat16)
        else:
            part[x * ny + y] = value

    every_cell(force_cell)

    for way in (2, 3):

        @pl.when(beside[behind[way]][0])
        def _():
            copy_x(dilated, 1, way).wait_recv()

        x, halo, d = edge_x(0, way)
        for y in range(ny):
            value = part[x * ny + y] + flag(d, x, y) * dilated[halo, y + 1].astype(jnp.float32) * (
                STEP_SIZE * STATE_STIFFNESS
            )
            if 0 < y < ny - 1:
                moved[x, y] = value.astype(jnp.bfloat16)
            else:
                part[x * ny + y] = value

    for chunk in order:
        for way, y, halo, d in ((0, 0, 0, 4), (1, ny - 1, ny + 1, 1)):

            @pl.when(beside[behind[way]][0])
            def _():
                copy_y(dilated, 1, way, chunk).wait_recv()

            for i in range(piece):
                x = chunk * piece + i
                value = part[x * ny + y] + flag(d, x, y) * dilated[x + 1, halo].astype(
                    jnp.float32
                ) * (STEP_SIZE * STATE_STIFFNESS)
                moved[x, y] = value.astype(jnp.bfloat16)

    for turn, buffer in enumerate((field, dilated)):
        for way in (0, 1):
            for chunk in order:

                @pl.when(beside[way][0])
                def _():
                    copy_y(buffer, turn, way, chunk).wait_send()

        for way in (2, 3):

            @pl.when(beside[way][0])
            def _():
                copy_x(buffer, turn, way).wait_send()


def mechanics(bricks, displacement, bonds):
    nx, ny, length, cases = displacement.shape
    vmem = pl.BlockSpec(memory_space=pltpu.VMEM)
    dma = pltpu.SemaphoreType.DMA
    padded = pltpu.VMEM((nx + 2, ny + 2, length, cases), jnp.bfloat16)
    return pl.pallas_call(
        mechanics_kernel,
        out_shape=jax.ShapeDtypeStruct(displacement.shape, jnp.bfloat16),
        in_specs=[vmem, vmem, vmem],
        out_specs=vmem,
        scratch_shapes=[
            pltpu.VMEM((6, nx * ny, length, cases), jnp.bfloat16),
            padded,
            padded,
            pltpu.VMEM((nx * ny, length, cases), jnp.float32),
            dma((2, 2, 2, HALO_CHUNKS)),
            dma((2, 2, 2)),
        ],
        compiler_params=pltpu.CompilerParams(
            collective_id=1, has_side_effects=True, vmem_limit_bytes=50 * MIB
        ),
        name="mechanics",
    )(bricks, displacement, bonds)


def local(
    heat_source,
    diagonal,
    active,
    conductance,
    pattern,
    send_list,
    owner_map,
    displacement,
    bond_live,
):
    blocks, tile_count, length = conductance.shape[:3]
    cases = heat_source.shape[1]
    devices = lax.axis_size(("row", "col"))
    me = lax.axis_index(("row", "col"))
    cap = max(1, blocks // devices)

    slots = jnp.arange(blocks, dtype=jnp.int32)
    mine = lax.dynamic_slice_in_dim(owner_map, me * blocks, blocks, axis=1)
    my_distance = (mine[0] - me + devices) % devices
    of_slot = mine[1][None, :] == slots[:, None]
    block_of = jnp.sum(jnp.where(of_slot, slots[None, :], 0), axis=1)
    distance = jnp.sum(jnp.where(of_slot, my_distance[None, :], 0), axis=1)
    rank = jnp.sum(
        ((distance[:, None] == distance[None, :]) & (slots[None, :] < slots[:, None])).astype(
            jnp.int32
        ),
        axis=1,
    )
    target = ((me + distance) % devices) * cap + rank
    places = jnp.arange(devices * cap, dtype=jnp.int32)
    route = jnp.sum(jnp.where(target[None, :] == places[:, None], block_of[None, :], 0), axis=1)
    source_row = ((me - distance + devices) % devices) * cap + rank

    bricks = curve(
        pattern,
        send_list,
        jnp.concatenate([route, source_row]),
        heat_source.reshape(blocks, length, cases),
        active.reshape(blocks, length),
        diagonal.reshape(blocks, length),
        conductance,
        devices,
    ).reshape(displacement.shape)
    moved = mechanics(bricks, displacement, bond_live.reshape(-1, length))
    return (bricks, moved)


def solution(mesh):
    return jax.shard_map(
        local,
        mesh=mesh,
        in_specs=(
            P(("row", "col"), None),
            P(("row", "col")),
            P(("row", "col")),
            P(("row", "col"), None, None, None),
            P(("row", "col"), None),
            P(("row", "col"), None, None),
            P(),
            P("row", "col", None, None),
            P(None, "row", "col", None),
        ),
        out_specs=(P("row", "col", None, None), P("row", "col", None, None)),
        check_vma=False,
    )
```

```python
import functools

import jax
import jax.numpy as jnp
from jax import lax
from jax.experimental import pallas as pl
from jax.experimental.pallas import tpu as pltpu
from jax.sharding import PartitionSpec as P

ITERS = 3
LOWER = 1.0
UPPER = 10.0
ALPHA_T = 0.5
BOND_STIFFNESS = 1.0
STATE_STIFFNESS = 2.0
STEP_SIZE = 0.1
GHOST_STEPS = (1, -1, 2, -2)
SEND_ORDER = (2, 3, 0, 1)
Z_CHUNKS = 4
ROW_TILE = 16
MESH = pl.DeviceIdType.MESH
MIB = 1024 * 1024


def chebyshev_weights(count):
    center = (UPPER + LOWER) / 2.0
    half_width = (UPPER - LOWER) / 2.0
    ratio_value = center / half_width
    previous = 1.0 / ratio_value
    weights = []
    for step_number in range(count):
        current = 1.0 / (2.0 * ratio_value - previous)
        weights.append((current * previous, 2.0 * current / half_width))
        previous = current
    return (1.0 / center, weights)


def fused_kernel(
    ny,
    pattern,
    send_list,
    table,
    heat_hbm,
    active,
    diagonal,
    conductance,
    displacement,
    bonds,
    bricks,
    moved,
    tiles,
    brick_field,
    ext0,
    ext1,
    ext2,
    outgoing,
    residual,
    direction,
    total,
    active_wide,
    diagonal_wide,
    *rest,
):
    arrived = rest[:Z_CHUNKS]
    (
        tile_sem,
        heat_sem,
        bricks_sem,
        moved_sem,
        send_sem,
        recv_sem,
        out_sem,
        in_sem,
        sem_y,
        sem_x,
    ) = rest[Z_CHUNKS:]
    rows, cols = lax.axis_size("row"), lax.axis_size("col")
    devices = rows * cols
    row, col = lax.axis_index("row"), lax.axis_index("col")
    me = row * cols + col
    blocks, length, cases = brick_field.shape
    tile_count = tiles.shape[1]
    cap = send_list.shape[2]
    ghosts = cap * len(GHOST_STEPS)
    places = arrived[0].shape[0]
    share = places // devices
    exts = (ext0, ext1, ext2)
    first_scale, weights = chebyshev_weights(ITERS)

    heat = brick_field
    heat_copy = pltpu.make_async_copy(heat_hbm, heat, heat_sem)
    heat_copy.start()
    tile_copy = pltpu.make_async_copy(conductance, tiles, tile_sem)
    tile_copy.start()

    def inside(index):
        return jnp.logical_and(index >= 0, index < devices)

    def place(index):
        return (lax.div(index, cols), lax.rem(index, cols))

    barrier = pltpu.get_barrier_semaphore()

    @pl.loop(1, devices)
    def _(i):
        peer = lax.rem(me + i, devices)
        pl.semaphore_signal(barrier, inc=1, device_id=place(peer), device_id_type=MESH)

    def ghost_copy(it, group):
        return pltpu.make_async_remote_copy(
            src_ref=outgoing.at[pl.ds((it % 2) * ghosts + group * cap, cap)],
            dst_ref=exts[it].at[pl.ds(blocks + group * cap, cap)],
            send_sem=send_sem.at[it, group],
            recv_sem=recv_sem.at[it, group],
            device_id=place(me + GHOST_STEPS[group]),
            device_id_type=MESH,
        )

    wide = jnp.concatenate([active[...].astype(jnp.float32), diagonal[...]], axis=0).T
    for b in range(blocks):
        column = jnp.broadcast_to(wide[:, b : b + 1], (length, cases))
        active_wide[b] = column.astype(jnp.bfloat16)

    heat_copy.wait()

    def first_value(b):
        start = heat[b].astype(jnp.float32) * first_scale
        return (start * active_wide[b].astype(jnp.float32)).astype(jnp.bfloat16)

    for group in SEND_ORDER:

        @pl.loop(0, cap)
        def _(j):
            outgoing[group * cap + j] = first_value(send_list[0, group, j])

        if group == SEND_ORDER[0]:
            pl.semaphore_wait(barrier, devices - 1)

        @pl.when(inside(me + GHOST_STEPS[group]))
        def _():
            ghost_copy(0, group).start()

    for it in range(ITERS):
        for group, step in enumerate(GHOST_STEPS):

            @pl.when(jnp.logical_not(inside(me - step)))
            def _():
                exts[it][pl.ds(blocks + group * cap, cap)] = jnp.zeros(
                    (cap, length, cases), jnp.bfloat16
                )

    for b in range(blocks):
        diagonal_wide[b] = jnp.broadcast_to(
            wide[:, blocks + b : blocks + b + 1], (length, cases)
        )

    @pl.loop(0, blocks)
    def _(b):
        source = heat[b].astype(jnp.float32)
        residual[b] = source
        direction[b] = source * first_scale
        ext0[b] = first_value(b)

    field_copy = pltpu.make_async_copy(displacement, brick_field, heat_sem)
    field_copy.start()
    tile_copy.wait()

    for it in range(ITERS):
        ext = exts[it]
        old_weight, res_weight = weights[it]
        last = it == ITERS - 1

        @pl.loop(0, blocks)
        def _(b):
            own = jnp.dot(tiles[b, 0], ext[b], preferred_element_type=jnp.float32)
            held = direction[b]
            left = (
                residual[b] - diagonal_wide[b] * held - active_wide[b].astype(jnp.float32) * own
            )
            mixed = old_weight * held + res_weight * left
            summed = held if it == 0 else total[b] + held
            if last:
                total[b] = summed + mixed
            else:
                residual[b] = left
                direction[b] = mixed
                total[b] = summed

        for group, step in enumerate(GHOST_STEPS):

            @pl.when(inside(me - step))
            def _():
                ghost_copy(it, group).wait_recv()

        def far_of(b):
            chosen = [ext[blocks + b]]
            for k in range(2, tile_count):
                chosen.append(ext[pattern[k, b]])
            line = jnp.concatenate([tiles[b, k] for k in range(1, tile_count)], axis=1)
            far = jnp.dot(line, jnp.concatenate(chosen, axis=0), preferred_element_type=jnp.float32)
            return active_wide[b].astype(jnp.float32) * far

        if last:
            break
        for group in SEND_ORDER:
            if it > 0:

                @pl.when(inside(me + GHOST_STEPS[group]))
                def _():
                    ghost_copy(it - 1, group).wait_send()

            @pl.loop(0, cap, unroll=2)
            def _(j):
                b = send_list[0, group, j]
                value = direction[b] - res_weight * far_of(b)
                outgoing[(it + 1) % 2 * ghosts + group * cap + j] = (
                    value * active_wide[b].astype(jnp.float32)
                ).astype(jnp.bfloat16)

            @pl.when(inside(me + GHOST_STEPS[group]))
            def _():
                ghost_copy(it + 1, group).start()

        @pl.loop(0, blocks, unroll=2)
        def _(b):
            far = far_of(b)
            residual[b] = residual[b] - far
            held = direction[b] - res_weight * far
            direction[b] = held
            exts[it + 1][b] = (held * active_wide[b].astype(jnp.float32)).astype(jnp.bfloat16)

    depth = length // Z_CHUNKS
    spare = ITERS % 2 * ghosts

    def levels(c):
        return pl.ds(c * depth, depth)

    def brick_copy(c, target, source):
        return pltpu.make_async_remote_copy(
            src_ref=outgoing.at[pl.ds(spare + target * share, share), levels(c)],
            dst_ref=arrived[c].at[pl.ds(source * share, share)],
            send_sem=out_sem.at[c, target],
            recv_sem=in_sem.at[c, source],
            device_id=place(target),
            device_id_type=MESH,
        )

    for group, step in enumerate(GHOST_STEPS):

        @pl.when(inside(me + step))
        def _():
            ghost_copy(ITERS - 2, group).wait_send()

    def final(b):
        return (total[b] - res_weight * far_of(b)).astype(jnp.bfloat16)

    @pl.loop(1, devices)
    def _(i):
        target = lax.rem(me + i, devices)
        for r in range(share):
            outgoing[spare + target * share + r] = final(table[target * share + r])
        brick_copy(0, target, me).start()

    for r in range(share):
        value = final(table[me * share + r])
        for c in range(Z_CHUNKS):
            arrived[c][me * share + r] = value[c * depth : (c + 1) * depth]

    nx = blocks // ny
    span = nx + 2
    field, dilated, held_bricks, part, live = ext0, ext1, ext2, residual, tiles
    scale = ALPHA_T * 0.5

    def at(x, y):
        return (y + 1) * span + x + 1

    beside = (
        (col + 1 < cols, (row, col + 1)),
        (col > 0, (row, col - 1)),
        (row + 1 < rows, (row + 1, col)),
        (row > 0, (row - 1, col)),
    )
    behind = (1, 0, 3, 2)

    def halo_copies(buffer, turn, c, way):
        def copy(source, target, size, sem):
            return pltpu.make_async_remote_copy(
                src_ref=buffer.at[pl.ds(source, size), levels(c)],
                dst_ref=buffer.at[pl.ds(target, size), levels(c)],
                send_sem=sem.at[0],
                recv_sem=sem.at[1],
                device_id=beside[way][1],
                device_id_type=MESH,
            )

        if way == 0:
            return [copy(at(0, ny - 1), at(0, -1), nx, sem_y.at[turn, c, way])]
        if way == 1:
            return [copy(at(0, 0), at(0, ny), nx, sem_y.at[turn, c, way])]
        if way == 2:
            ends = (nx - 1, -1)
        else:
            ends = (0, nx)
        return [
            copy(at(ends[0], y), at(ends[1], y), 1, sem_x.at[turn, c, way - 2, y])
            for y in range(ny)
        ]

    def send_halo(buffer, turn, c, way):
        @pl.when(beside[way][0])
        def _():
            for copy in halo_copies(buffer, turn, c, way):
                copy.start()

    def wait_halo(buffer, turn, c, way):
        @pl.when(beside[behind[way]][0])
        def _():
            for copy in halo_copies(buffer, turn, c, way):
                copy.wait_recv()

    for buffer in (field, dilated):
        for way, start, size in ((0, at(0, -1), nx), (1, at(0, ny), nx)):

            @pl.when(jnp.logical_not(beside[behind[way]][0]))
            def _():
                buffer[pl.ds(start, size)] = jnp.zeros((size, length, cases), jnp.bfloat16)

        for way, x in ((2, -1), (3, nx)):

            @pl.when(jnp.logical_not(beside[behind[way]][0]))
            def _():
                for y in range(ny):
                    buffer[at(x, y)] = jnp.zeros((length, cases), jnp.bfloat16)

    for half in range(3):
        flags = bonds[pl.ds(half * 2 * blocks, 2 * blocks)].astype(jnp.float32).T
        for j in range(2 * blocks):
            live[j % blocks, half * 2 + j // blocks] = jnp.broadcast_to(
                flags[:, j : j + 1], (length, cases)
            ).astype(jnp.bfloat16)

    field_copy.wait()

    def edges_first(body, ready):
        @pl.loop(0, nx, unroll=2)
        def _(x):
            body(x, 0)
            body(x, ny - 1)

        ready(0)
        ready(1)
        for y in range(1, ny - 1):
            body(0, y)
            body(nx - 1, y)

        ready(2)
        ready(3)

        @pl.loop(1, nx - 1, unroll=2)
        def _(x):
            for y in range(1, ny - 1):
                body(x, y)

    def receive(c):
        def cell(x, y):
            b = x * ny + y
            value = arrived[c][table[places + b]]
            held_bricks[b, levels(c)] = value
            moving = brick_field[b, levels(c)].astype(jnp.float32)
            field[at(x, y), levels(c)] = (moving - scale * value.astype(jnp.float32)).astype(
                jnp.bfloat16
            )

        edges_first(cell, lambda way: send_halo(field, 0, c, way))

    def stencil(buffer, c, x, y):
        low = max(c * depth - ROW_TILE, 0)
        high = min((c + 1) * depth + ROW_TILE, length)
        inner = slice(c * depth - low, (c + 1) * depth - low)
        b = x * ny + y
        centre = buffer[at(x, y), pl.ds(low, high - low)].astype(jnp.float32)
        terms = (
            (2, pltpu.roll(centre, high - low - 1, 0)[inner]),
            (5, pltpu.roll(centre, 1, 0)[inner]),
            (0, buffer[at(x + 1, y), levels(c)].astype(jnp.float32)),
            (3, buffer[at(x - 1, y), levels(c)].astype(jnp.float32)),
            (1, buffer[at(x, y + 1), levels(c)].astype(jnp.float32)),
            (4, buffer[at(x, y - 1), levels(c)].astype(jnp.float32)),
        )
        summed = count = None
        for d, value in terms:
            bond = live[b, d, levels(c)].astype(jnp.float32)
            summed = bond * value if summed is None else summed + bond * value
            count = bond if count is None else count + bond
        return summed, count

    def dilate(c):
        for way in range(4):
            wait_halo(field, 0, c, way)

        def cell(x, y):
            b = x * ny + y
            summed, count = stencil(field, c, x, y)
            moving = brick_field[b, levels(c)].astype(jnp.float32)
            warm = scale * held_bricks[b, levels(c)].astype(jnp.float32)
            value = (summed - count * (moving + warm)) * (1.0 / 6.0)
            part[b, levels(c)] = value
            dilated[at(x, y), levels(c)] = value.astype(jnp.bfloat16)

        edges_first(cell, lambda way: send_halo(dilated, 1, c, way))

    def moved_copy(c):
        return pltpu.make_async_copy(
            brick_field.at[:, levels(c)], moved.at[:, levels(c)], moved_sem.at[c]
        )

    def move(c):
        for way in range(4):
            wait_halo(dilated, 1, c, way)

        @pl.loop(0, nx, unroll=2)
        def _(x):
            for y in range(ny):
                b = x * ny + y
                summed, count = stencil(dilated, c, x, y)
                centre = part[b, levels(c)]
                force = BOND_STIFFNESS * 6.0 * centre + STATE_STIFFNESS * (summed - count * centre)
                moving = brick_field[b, levels(c)].astype(jnp.float32)
                brick_field[b, levels(c)] = (moving + STEP_SIZE * force).astype(jnp.bfloat16)

        moved_copy(c).start()

    bricks_copy = pltpu.make_async_copy(held_bricks.at[pl.ds(0, blocks)], bricks, bricks_sem)
    for step in range(Z_CHUNKS + 2):
        if step < Z_CHUNKS:

            @pl.loop(1, devices)
            def _(i):
                target = lax.rem(me + i, devices)
                brick_copy(step, target, me).wait_send()
                if step + 1 < Z_CHUNKS:
                    brick_copy(step + 1, target, me).start()

            @pl.loop(1, devices)
            def _(i):
                brick_copy(step, me, lax.rem(me + devices - i, devices)).wait_recv()

            receive(step)
            if step == Z_CHUNKS - 1:
                bricks_copy.start()
        if 1 <= step <= Z_CHUNKS:
            dilate(step - 1)
        if step >= 2:
            move(step - 2)

    for group, step in enumerate(GHOST_STEPS):

        @pl.when(inside(me + step))
        def _():
            ghost_copy(ITERS - 1, group).wait_send()

    for turn, buffer in enumerate((field, dilated)):
        for c in range(Z_CHUNKS):
            for way in range(4):

                @pl.when(beside[way][0])
                def _():
                    for copy in halo_copies(buffer, turn, c, way):
                        copy.wait_send()

    bricks_copy.wait()
    for c in range(Z_CHUNKS):
        moved_copy(c).wait()


def fused(pattern, send_list, table, heat, active, diagonal, conductance, displacement, bonds, devices, ny):
    blocks, length, cases = heat.shape
    ghosts = send_list.shape[1] * send_list.shape[2]
    places = table.shape[0] - blocks
    smem = pl.BlockSpec(memory_space=pltpu.SMEM)
    vmem = pl.BlockSpec(memory_space=pltpu.VMEM)
    hbm = pl.BlockSpec(memory_space=pl.ANY)
    state = pltpu.VMEM((blocks, length, cases), jnp.float32)
    ext = pltpu.VMEM((max(blocks + ghosts, (blocks // ny + 2) * (ny + 2)), length, cases), jnp.bfloat16)
    half = pltpu.VMEM((blocks, length, cases), jnp.bfloat16)
    dma = pltpu.SemaphoreType.DMA
    result = jax.ShapeDtypeStruct((blocks, length, cases), jnp.bfloat16)
    return pl.pallas_call(
        functools.partial(fused_kernel, ny),
        out_shape=(result, result),
        in_specs=[smem, smem, smem, hbm, vmem, vmem, hbm, hbm, vmem],
        out_specs=(hbm, hbm),
        scratch_shapes=[
            pltpu.VMEM(conductance.shape, jnp.bfloat16),
            half,
            ext,
            ext,
            ext,
            pltpu.VMEM((ghosts + max(ghosts, places), length, cases), jnp.bfloat16),
            state,
            state,
            state,
            half,
            state,
            *[pltpu.VMEM((places, length // Z_CHUNKS, cases), jnp.bfloat16)] * Z_CHUNKS,
            dma,
            dma,
            dma,
            dma((Z_CHUNKS,)),
            dma((ITERS, len(GHOST_STEPS))),
            dma((ITERS, len(GHOST_STEPS))),
            dma((Z_CHUNKS, devices)),
            dma((Z_CHUNKS, devices)),
            dma((2, Z_CHUNKS, 2, 2)),
            dma((2, Z_CHUNKS, 2, ny, 2)),
        ],
        compiler_params=pltpu.CompilerParams(
            collective_id=0, has_side_effects=True, vmem_limit_bytes=60 * MIB
        ),
        name="fused",
    )(pattern, send_list, table, heat, active, diagonal, conductance, displacement, bonds)


def local(
    heat_source,
    diagonal,
    active,
    conductance,
    pattern,
    send_list,
    owner_map,
    displacement,
    bond_live,
):
    blocks, tile_count, length = conductance.shape[:3]
    cases = heat_source.shape[1]
    devices = lax.axis_size(("row", "col"))
    me = lax.axis_index(("row", "col"))
    cap = max(1, blocks // devices)

    slots = jnp.arange(blocks, dtype=jnp.int32)
    mine = lax.dynamic_slice_in_dim(owner_map, me * blocks, blocks, axis=1)
    my_distance = (mine[0] - me + devices) % devices
    of_slot = mine[1][None, :] == slots[:, None]
    block_of = jnp.sum(jnp.where(of_slot, slots[None, :], 0), axis=1)
    distance = jnp.sum(jnp.where(of_slot, my_distance[None, :], 0), axis=1)
    rank = jnp.sum(
        ((distance[:, None] == distance[None, :]) & (slots[None, :] < slots[:, None])).astype(
            jnp.int32
        ),
        axis=1,
    )
    target = ((me + distance) % devices) * cap + rank
    places = jnp.arange(devices * cap, dtype=jnp.int32)
    route = jnp.sum(jnp.where(target[None, :] == places[:, None], block_of[None, :], 0), axis=1)
    source_row = ((me - distance + devices) % devices) * cap + rank

    bricks, moved = fused(
        pattern.T,
        send_list,
        jnp.concatenate([route, source_row]),
        heat_source.reshape(blocks, length, cases),
        active.reshape(blocks, length),
        diagonal.reshape(blocks, length),
        conductance,
        displacement.reshape(blocks, length, cases),
        bond_live.reshape(-1, length),
        devices,
        displacement.shape[1],
    )
    return (bricks.reshape(displacement.shape), moved.reshape(displacement.shape))


def solution(mesh):
    return jax.shard_map(
        local,
        mesh=mesh,
        in_specs=(
            P(("row", "col"), None),
            P(("row", "col")),
            P(("row", "col")),
            P(("row", "col"), None, None, None),
            P(("row", "col"), None),
            P(("row", "col"), None, None),
            P(),
            P("row", "col", None, None),
            P(None, "row", "col", None),
        ),
        out_specs=(P("row", "col", None, None), P("row", "col", None, None)),
        check_vma=False,
    )
```

```python
import functools

import jax
import jax.numpy as jnp
from jax import lax
from jax.experimental import pallas as pl
from jax.experimental.pallas import tpu as pltpu
from jax.sharding import PartitionSpec as P

ITERS = 3
LOWER = 1.0
UPPER = 10.0
ALPHA_T = 0.5
BOND_STIFFNESS = 1.0
STATE_STIFFNESS = 2.0
STEP_SIZE = 0.1
GHOST_STEPS = (1, -1, 2, -2)
SEND_ORDER = (2, 3, 0, 1)
Z_SHARES = (2, 2, 2, 2)
Z_CHUNKS = len(Z_SHARES)
PIECES = 4
LANES = 128
ROW_TILE = 16
MESH = pl.DeviceIdType.MESH
MIB = 1024 * 1024


def chebyshev_weights(count):
    center = (UPPER + LOWER) / 2.0
    half_width = (UPPER - LOWER) / 2.0
    ratio_value = center / half_width
    previous = 1.0 / ratio_value
    weights = []
    for step_number in range(count):
        current = 1.0 / (2.0 * ratio_value - previous)
        weights.append((current * previous, 2.0 * current / half_width))
        previous = current
    return (1.0 / center, weights)


def fused_kernel(
    ny,
    pattern,
    send_list,
    owner_map,
    heat_hbm,
    active,
    diagonal,
    conductance,
    displacement,
    bonds,
    bricks,
    moved,
    tiles,
    ext0,
    ext1,
    ext2,
    outgoing,
    residual,
    direction,
    total,
    active_wide,
    diagonal_wide,
    table_rows,
    table,
    *rest,
):
    arrived = rest[:Z_CHUNKS]
    (
        tile_sem,
        heat_sem,
        table_sem,
        send_sem,
        recv_sem,
        out_sem,
        in_sem,
        sem_y,
        sem_x,
    ) = rest[Z_CHUNKS:]
    rows, cols = lax.axis_size("row"), lax.axis_size("col")
    devices = rows * cols
    row, col = lax.axis_index("row"), lax.axis_index("col")
    me = row * cols + col
    brick_field = moved
    blocks, length, cases = brick_field.shape
    tile_count = tiles.shape[1]
    cap = send_list.shape[2]
    ghosts = cap * len(GHOST_STEPS)
    places = arrived[0].shape[0]
    share = places // devices
    exts = (ext0, ext1, ext2)
    first_scale, weights = chebyshev_weights(ITERS)

    heat = brick_field
    heat_copy = pltpu.make_async_copy(heat_hbm, heat, heat_sem)
    heat_copy.start()
    tile_copy = pltpu.make_async_copy(conductance, tiles, tile_sem)
    tile_copy.start()

    def inside(index):
        return jnp.logical_and(index >= 0, index < devices)

    def place(index):
        return (lax.div(index, cols), lax.rem(index, cols))

    barrier = pltpu.get_barrier_semaphore()

    @pl.loop(1, devices)
    def _(i):
        peer = lax.rem(me + i, devices)
        pl.semaphore_signal(barrier, inc=1, device_id=place(peer), device_id_type=MESH)

    piece = cap // PIECES

    def ghost_copy(it, group, part):
        first = group * cap + part * piece
        return pltpu.make_async_remote_copy(
            src_ref=outgoing.at[pl.ds((it % 2) * ghosts + first, piece)],
            dst_ref=exts[it].at[pl.ds(blocks + first, piece)],
            send_sem=send_sem.at[it, group, part],
            recv_sem=recv_sem.at[it, group, part],
            device_id=place(me + GHOST_STEPS[group]),
            device_id_type=MESH,
        )

    wide = jnp.concatenate([active[...].astype(jnp.float32), diagonal[...]], axis=0).T
    for b in range(blocks):
        column = jnp.broadcast_to(wide[:, b : b + 1], (length, cases))
        active_wide[b] = column.astype(jnp.bfloat16)

    heat_copy.wait()

    def first_value(b):
        start = heat[b].astype(jnp.float32) * first_scale
        return (start * active_wide[b].astype(jnp.float32)).astype(jnp.bfloat16)

    def wait_sent(it):
        for group, step in enumerate(GHOST_STEPS):

            @pl.when(inside(me + step))
            def _():
                for part in range(PIECES):
                    ghost_copy(it, group, part).wait_send()

    def send_ghosts(it, value_of):
        @pl.loop(0, PIECES)
        def _(part):
            for group in SEND_ORDER:
                for i in range(piece):
                    j = part * piece + i
                    outgoing[it % 2 * ghosts + group * cap + j] = value_of(send_list[0, group, j])

                @pl.when(inside(me + GHOST_STEPS[group]))
                def _():
                    ghost_copy(it, group, part).start()

    pl.semaphore_wait(barrier, devices - 1)
    send_ghosts(0, first_value)

    for it in range(ITERS):
        for group, step in enumerate(GHOST_STEPS):

            @pl.when(jnp.logical_not(inside(me - step)))
            def _():
                exts[it][pl.ds(blocks + group * cap, cap)] = jnp.zeros(
                    (cap, length, cases), jnp.bfloat16
                )

    for b in range(blocks):
        diagonal_wide[b] = jnp.broadcast_to(
            wide[:, blocks + b : blocks + b + 1], (length, cases)
        )

    @pl.loop(0, blocks)
    def _(b):
        source = heat[b].astype(jnp.float32)
        residual[b] = source
        direction[b] = source * first_scale
        ext0[b] = first_value(b)

    first = lax.rem(me * blocks, LANES)
    aligned = pl.multiple_of(me * blocks - first, LANES)
    window = owner_map[:, pl.ds(aligned, LANES)]
    mine = window[:, :blocks]
    for start in range(blocks, LANES, blocks):
        mine = jnp.where(first == start, window[:, start : start + blocks], mine)
    down_rows = lax.broadcasted_iota(jnp.int32, (blocks, LANES), 0)
    along = lax.broadcasted_iota(jnp.int32, (blocks, LANES), 1)
    small_rows = lax.broadcasted_iota(jnp.int32, (blocks, blocks), 0)
    small_along = lax.broadcasted_iota(jnp.int32, (blocks, blocks), 1)
    away = lax.rem(mine[0:1] - me + devices, devices)
    of_slot = mine[1:2] == small_rows
    block_of = jnp.sum(jnp.where(of_slot, small_along, 0), axis=1, keepdims=True)
    distance = jnp.sum(jnp.where(of_slot, away, 0), axis=1, keepdims=True)
    distance_row = jnp.sum(
        jnp.where(small_rows == small_along, distance, 0), axis=0, keepdims=True
    )
    before = jnp.logical_and(distance == distance_row, small_along < small_rows)
    rank = jnp.sum(jnp.where(before, 1, 0), axis=1, keepdims=True)
    target_place = lax.rem(me + distance, devices) * share + rank
    source_place = lax.rem(me - distance + devices, devices) * share + rank
    table_rows[...] = jnp.zeros(table_rows.shape, jnp.int32)
    sent = jnp.sum(jnp.where(target_place == along, block_of, 0), axis=0, keepdims=True)
    held = jnp.sum(jnp.where(down_rows == along, source_place, 0), axis=0, keepdims=True)
    table_rows[0:1] = jnp.clip(sent, 0, blocks - 1)
    table_rows[1:2] = jnp.clip(held, 0, places - 1)
    table_copy = pltpu.make_async_copy(table_rows, table, table_sem)
    table_copy.start()

    field_copy = pltpu.make_async_copy(displacement, brick_field, heat_sem)
    field_copy.start()
    tile_copy.wait()

    for it in range(ITERS):
        ext = exts[it]
        old_weight, res_weight = weights[it]
        last = it == ITERS - 1

        @pl.loop(0, blocks)
        def _(b):
            own = jnp.dot(tiles[b, 0], ext[b], preferred_element_type=jnp.float32)
            held = direction[b]
            left = (
                residual[b] - diagonal_wide[b] * held - active_wide[b].astype(jnp.float32) * own
            )
            mixed = old_weight * held + res_weight * left
            summed = held if it == 0 else total[b] + held
            if last:
                total[b] = summed + mixed
            else:
                residual[b] = left
                direction[b] = mixed
                total[b] = summed

        for group, step in enumerate(GHOST_STEPS):

            @pl.when(inside(me - step))
            def _():
                for part in range(PIECES):
                    ghost_copy(it, group, part).wait_recv()

        def far_of(b):
            chosen = [ext[blocks + b]]
            for k in range(2, tile_count):
                chosen.append(ext[pattern[k, b]])
            line = jnp.concatenate([tiles[b, k] for k in range(1, tile_count)], axis=1)
            far = jnp.dot(line, jnp.concatenate(chosen, axis=0), preferred_element_type=jnp.float32)
            return active_wide[b].astype(jnp.float32) * far

        if last:
            break
        if it > 0:
            wait_sent(it - 1)

        def next_value(b):
            value = direction[b] - res_weight * far_of(b)
            return (value * active_wide[b].astype(jnp.float32)).astype(jnp.bfloat16)

        send_ghosts(it + 1, next_value)

        @pl.loop(0, blocks, unroll=2)
        def _(b):
            far = far_of(b)
            residual[b] = residual[b] - far
            held = direction[b] - res_weight * far
            direction[b] = held
            exts[it + 1][b] = (held * active_wide[b].astype(jnp.float32)).astype(jnp.bfloat16)

    unit = length // sum(Z_SHARES)
    starts = [unit * sum(Z_SHARES[:c]) for c in range(Z_CHUNKS + 1)]
    spare = ITERS % 2 * ghosts

    def levels(c):
        return pl.ds(starts[c], starts[c + 1] - starts[c])

    def brick_copy(c, target, source):
        return pltpu.make_async_remote_copy(
            src_ref=outgoing.at[pl.ds(spare + target * share, share), levels(c)],
            dst_ref=arrived[c].at[pl.ds(source * share, share)],
            send_sem=out_sem.at[c, target],
            recv_sem=in_sem.at[c, source],
            device_id=place(target),
            device_id_type=MESH,
        )

    wait_sent(ITERS - 2)
    table_copy.wait()

    def final(b):
        return (total[b] - res_weight * far_of(b)).astype(jnp.bfloat16)

    @pl.loop(1, devices)
    def _(i):
        target = lax.rem(me + i, devices)
        for r in range(share):
            outgoing[spare + target * share + r] = final(table[0, target * share + r])
        brick_copy(0, target, me).start()

    for r in range(share):
        value = final(table[0, me * share + r])
        for c in range(Z_CHUNKS):
            arrived[c][me * share + r] = value[starts[c] : starts[c + 1]]

    nx = blocks // ny
    span = nx + 2
    field, dilated, held_bricks, part, live = ext0, ext1, bricks, residual, tiles
    scale = ALPHA_T * 0.5

    def at(x, y):
        return (y + 1) * span + x + 1

    beside = (
        (col + 1 < cols, (row, col + 1)),
        (col > 0, (row, col - 1)),
        (row + 1 < rows, (row + 1, col)),
        (row > 0, (row - 1, col)),
    )
    behind = (1, 0, 3, 2)

    def halo_copies(buffer, turn, c, way):
        def copy(source, target, size, sem):
            return pltpu.make_async_remote_copy(
                src_ref=buffer.at[pl.ds(source, size), levels(c)],
                dst_ref=buffer.at[pl.ds(target, size), levels(c)],
                send_sem=sem.at[0],
                recv_sem=sem.at[1],
                device_id=beside[way][1],
                device_id_type=MESH,
            )

        if way == 0:
            return [copy(at(0, ny - 1), at(0, -1), nx, sem_y.at[turn, c, way])]
        if way == 1:
            return [copy(at(0, 0), at(0, ny), nx, sem_y.at[turn, c, way])]
        if way == 2:
            ends = (nx - 1, -1)
        else:
            ends = (0, nx)
        return [
            copy(at(ends[0], y), at(ends[1], y), 1, sem_x.at[turn, c, way - 2, y])
            for y in range(ny)
        ]

    def send_halo(buffer, turn, c, way):
        @pl.when(beside[way][0])
        def _():
            for copy in halo_copies(buffer, turn, c, way):
                copy.start()

    def wait_halo(buffer, turn, c, way):
        @pl.when(beside[behind[way]][0])
        def _():
            for copy in halo_copies(buffer, turn, c, way):
                copy.wait_recv()

    for buffer in (field, dilated):
        for way, start, size in ((0, at(0, -1), nx), (1, at(0, ny), nx)):

            @pl.when(jnp.logical_not(beside[behind[way]][0]))
            def _():
                buffer[pl.ds(start, size)] = jnp.zeros((size, length, cases), jnp.bfloat16)

        for way, x in ((2, -1), (3, nx)):

            @pl.when(jnp.logical_not(beside[behind[way]][0]))
            def _():
                for y in range(ny):
                    buffer[at(x, y)] = jnp.zeros((length, cases), jnp.bfloat16)

    for half in range(3):
        flags = bonds[pl.ds(half * 2 * blocks, 2 * blocks)].astype(jnp.float32).T
        for j in range(2 * blocks):
            live[j % blocks, half * 2 + j // blocks] = jnp.broadcast_to(
                flags[:, j : j + 1], (length, cases)
            ).astype(jnp.bfloat16)

    field_copy.wait()

    def edges(body, ready):
        @pl.loop(0, nx, unroll=2)
        def _(x):
            body(x, 0)
            body(x, ny - 1)

        ready(0)
        ready(1)
        for y in range(1, ny - 1):
            body(0, y)
            body(nx - 1, y)

        ready(2)
        ready(3)

    def inside_cells(body):
        @pl.loop(1, nx - 1, unroll=2)
        def _(x):
            for y in range(1, ny - 1):
                body(x, y)

    def receive(c):
        def cell(x, y):
            b = x * ny + y
            value = arrived[c][table[1, b]]
            held_bricks[b, levels(c)] = value
            moving = brick_field[b, levels(c)].astype(jnp.float32)
            field[at(x, y), levels(c)] = (moving - scale * value.astype(jnp.float32)).astype(
                jnp.bfloat16
            )

        edges(cell, lambda way: send_halo(field, 0, c, way))
        inside_cells(cell)

    def stencil(buffer, c, x, y):
        low = max(starts[c] - ROW_TILE, 0)
        high = min(starts[c + 1] + ROW_TILE, length)
        inner = slice(starts[c] - low, starts[c + 1] - low)
        b = x * ny + y
        centre = buffer[at(x, y), pl.ds(low, high - low)].astype(jnp.float32)
        terms = (
            (2, pltpu.roll(centre, high - low - 1, 0)[inner]),
            (5, pltpu.roll(centre, 1, 0)[inner]),
            (0, buffer[at(x + 1, y), levels(c)].astype(jnp.float32)),
            (3, buffer[at(x - 1, y), levels(c)].astype(jnp.float32)),
            (1, buffer[at(x, y + 1), levels(c)].astype(jnp.float32)),
            (4, buffer[at(x, y - 1), levels(c)].astype(jnp.float32)),
        )
        summed = count = None
        for d, value in terms:
            bond = live[b, d, levels(c)].astype(jnp.float32)
            summed = bond * value if summed is None else summed + bond * value
            count = bond if count is None else count + bond
        return summed, count

    def dilate(c):
        def cell(x, y):
            b = x * ny + y
            summed, count = stencil(field, c, x, y)
            moving = brick_field[b, levels(c)].astype(jnp.float32)
            warm = scale * held_bricks[b, levels(c)].astype(jnp.float32)
            value = (summed - count * (moving + warm)) * (1.0 / 6.0)
            part[b, levels(c)] = value
            dilated[at(x, y), levels(c)] = value.astype(jnp.bfloat16)

        if c == Z_CHUNKS - 1:
            inside_cells(cell)
        for way in range(4):
            wait_halo(field, 0, c, way)
        edges(cell, lambda way: send_halo(dilated, 1, c, way))
        if c < Z_CHUNKS - 1:
            inside_cells(cell)

    def move(c):
        def cell(x, y):
            b = x * ny + y
            summed, count = stencil(dilated, c, x, y)
            centre = part[b, levels(c)]
            force = BOND_STIFFNESS * 6.0 * centre + STATE_STIFFNESS * (summed - count * centre)
            moving = brick_field[b, levels(c)].astype(jnp.float32)
            brick_field[b, levels(c)] = (moving + STEP_SIZE * force).astype(jnp.bfloat16)

        inside_cells(cell)
        for way in range(4):
            wait_halo(dilated, 1, c, way)
        edges(cell, lambda way: None)

    for step in range(Z_CHUNKS + 2):
        if step < Z_CHUNKS:

            @pl.loop(1, devices)
            def _(i):
                target = lax.rem(me + i, devices)
                brick_copy(step, target, me).wait_send()
                if step + 1 < Z_CHUNKS:
                    brick_copy(step + 1, target, me).start()

            @pl.loop(1, devices)
            def _(i):
                brick_copy(step, me, lax.rem(me + devices - i, devices)).wait_recv()

            receive(step)
        if 1 <= step <= Z_CHUNKS:
            dilate(step - 1)
        if step >= 2:
            move(step - 2)

    wait_sent(ITERS - 1)

    for turn, buffer in enumerate((field, dilated)):
        for c in range(Z_CHUNKS):
            for way in range(4):

                @pl.when(beside[way][0])
                def _():
                    for copy in halo_copies(buffer, turn, c, way):
                        copy.wait_send()


def fused(pattern, send_list, owner_map, heat, active, diagonal, conductance, displacement, bonds, devices, ny):
    blocks, length, cases = heat.shape
    ghosts = send_list.shape[1] * send_list.shape[2]
    places = devices * max(1, blocks // devices)
    smem = pl.BlockSpec(memory_space=pltpu.SMEM)
    vmem = pl.BlockSpec(memory_space=pltpu.VMEM)
    hbm = pl.BlockSpec(memory_space=pl.ANY)
    state = pltpu.VMEM((blocks, length, cases), jnp.float32)
    ext = pltpu.VMEM((max(blocks + ghosts, (blocks // ny + 2) * (ny + 2)), length, cases), jnp.bfloat16)
    half = pltpu.VMEM((blocks, length, cases), jnp.bfloat16)
    dma = pltpu.SemaphoreType.DMA
    result = pltpu.VMEM((blocks, length, cases), jnp.bfloat16)
    return pl.pallas_call(
        functools.partial(fused_kernel, ny),
        out_shape=(result, result),
        in_specs=[smem, smem, vmem, hbm, vmem, vmem, hbm, hbm, vmem],
        out_specs=(vmem, vmem),
        scratch_shapes=[
            pltpu.VMEM(conductance.shape, jnp.bfloat16),
            ext,
            ext,
            ext,
            pltpu.VMEM((ghosts + max(ghosts, places), length, cases), jnp.bfloat16),
            state,
            state,
            state,
            half,
            state,
            pltpu.VMEM((8, LANES), jnp.int32),
            pltpu.SMEM((8, LANES), jnp.int32),
            *[
                pltpu.VMEM((places, length // sum(Z_SHARES) * share, cases), jnp.bfloat16)
                for share in Z_SHARES
            ],
            dma,
            dma,
            dma,
            dma((ITERS, len(GHOST_STEPS), PIECES)),
            dma((ITERS, len(GHOST_STEPS), PIECES)),
            dma((Z_CHUNKS, devices)),
            dma((Z_CHUNKS, devices)),
            dma((2, Z_CHUNKS, 2, 2)),
            dma((2, Z_CHUNKS, 2, ny, 2)),
        ],
        compiler_params=pltpu.CompilerParams(
            collective_id=0, has_side_effects=True, vmem_limit_bytes=57 * MIB
        ),
        name="fused",
    )(pattern, send_list, owner_map, heat, active, diagonal, conductance, displacement, bonds)


def local(
    heat_source,
    diagonal,
    active,
    conductance,
    pattern,
    send_list,
    owner_map,
    displacement,
    bond_live,
):
    blocks, tile_count, length = conductance.shape[:3]
    cases = heat_source.shape[1]
    devices = lax.axis_size(("row", "col"))

    bricks, moved = fused(
        pattern.T,
        send_list,
        owner_map,
        heat_source.reshape(blocks, length, cases),
        active.reshape(blocks, length),
        diagonal.reshape(blocks, length),
        conductance,
        displacement.reshape(blocks, length, cases),
        bond_live.reshape(-1, length),
        devices,
        displacement.shape[1],
    )
    return (bricks.reshape(displacement.shape), moved.reshape(displacement.shape))


def solution(mesh):
    return jax.shard_map(
        local,
        mesh=mesh,
        in_specs=(
            P(("row", "col"), None),
            P(("row", "col")),
            P(("row", "col")),
            P(("row", "col"), None, None, None),
            P(("row", "col"), None),
            P(("row", "col"), None, None),
            P(),
            P("row", "col", None, None),
            P(None, "row", "col", None),
        ),
        out_specs=(P("row", "col", None, None), P("row", "col", None, None)),
        check_vma=False,
    )
```

```python
import functools

import jax
import jax.numpy as jnp
from jax import lax
from jax.experimental import pallas as pl
from jax.experimental.pallas import tpu as pltpu
from jax.sharding import PartitionSpec as P

ITERS = 3
LOWER = 1.0
UPPER = 10.0
ALPHA_T = 0.5
BOND_STIFFNESS = 1.0
STATE_STIFFNESS = 2.0
STEP_SIZE = 0.1
GHOST_STEPS = (1, -1, 2, -2)
SEND_ORDER = (2, 3, 0, 1)
Z_SHARES = (2, 2, 2, 2)
Z_CHUNKS = len(Z_SHARES)
PIECES = 4
LANES = 128
ROW_TILE = 16
MESH = pl.DeviceIdType.MESH
MIB = 1024 * 1024


def chebyshev_weights(count):
    center = (UPPER + LOWER) / 2.0
    half_width = (UPPER - LOWER) / 2.0
    ratio_value = center / half_width
    previous = 1.0 / ratio_value
    weights = []
    for step_number in range(count):
        current = 1.0 / (2.0 * ratio_value - previous)
        weights.append((current * previous, 2.0 * current / half_width))
        previous = current
    return (1.0 / center, weights)


def fused_kernel(
    ny,
    pattern,
    send_list,
    owner_map,
    heat_hbm,
    active,
    diagonal,
    conductance,
    displacement,
    bonds,
    bricks,
    moved,
    tiles,
    ext0,
    ext1,
    ext2,
    outgoing,
    residual,
    direction,
    total,
    active_wide,
    diagonal_wide,
    table_rows,
    table,
    *rest,
):
    arrived = rest[:Z_CHUNKS]
    (
        tile_sem,
        heat_sem,
        table_sem,
        send_sem,
        recv_sem,
        out_sem,
        in_sem,
        sem_y,
        sem_x,
    ) = rest[Z_CHUNKS:]
    rows, cols = lax.axis_size("row"), lax.axis_size("col")
    devices = rows * cols
    row, col = lax.axis_index("row"), lax.axis_index("col")
    me = row * cols + col
    brick_field = moved
    blocks, length, cases = brick_field.shape
    tile_count = tiles.shape[1]
    cap = send_list.shape[2]
    ghosts = cap * len(GHOST_STEPS)
    places = arrived[0].shape[0]
    share = places // devices
    exts = (ext0, ext1, ext2)
    first_scale, weights = chebyshev_weights(ITERS)

    heat = brick_field
    heat_copy = pltpu.make_async_copy(heat_hbm, heat, heat_sem)
    heat_copy.start()
    tile_copy = pltpu.make_async_copy(conductance, tiles, tile_sem)

    def inside(index):
        return jnp.logical_and(index >= 0, index < devices)

    def place(index):
        return (lax.div(index, cols), lax.rem(index, cols))

    barrier = pltpu.get_barrier_semaphore()

    @pl.loop(1, devices)
    def _(i):
        peer = lax.rem(me + i, devices)
        pl.semaphore_signal(barrier, inc=1, device_id=place(peer), device_id_type=MESH)

    piece = cap // PIECES

    def ghost_copy(it, group, part):
        first = group * cap + part * piece
        return pltpu.make_async_remote_copy(
            src_ref=outgoing.at[pl.ds((it % 2) * ghosts + first, piece)],
            dst_ref=exts[it].at[pl.ds(blocks + first, piece)],
            send_sem=send_sem.at[it, group, part],
            recv_sem=recv_sem.at[it, group, part],
            device_id=place(me + GHOST_STEPS[group]),
            device_id_type=MESH,
        )

    wide = jnp.concatenate([active[...].astype(jnp.float32), diagonal[...]], axis=0).T
    for b in range(blocks):
        column = jnp.broadcast_to(wide[:, b : b + 1], (length, cases))
        active_wide[b] = column.astype(jnp.bfloat16)

    heat_copy.wait()

    def first_value(b):
        start = heat[b].astype(jnp.float32) * first_scale
        return (start * active_wide[b].astype(jnp.float32)).astype(jnp.bfloat16)

    def wait_sent(it):
        for group, step in enumerate(GHOST_STEPS):

            @pl.when(inside(me + step))
            def _():
                for part in range(PIECES):
                    ghost_copy(it, group, part).wait_send()

    def send_ghosts(it, value_of):
        @pl.loop(0, PIECES)
        def _(part):
            for group in SEND_ORDER:
                for i in range(piece):
                    j = part * piece + i
                    outgoing[it % 2 * ghosts + group * cap + j] = value_of(send_list[0, group, j])

                @pl.when(inside(me + GHOST_STEPS[group]))
                def _():
                    ghost_copy(it, group, part).start()

    pl.semaphore_wait(barrier, devices - 1)
    send_ghosts(0, first_value)
    tile_copy.start()

    for it in range(ITERS):
        for group, step in enumerate(GHOST_STEPS):

            @pl.when(jnp.logical_not(inside(me - step)))
            def _():
                exts[it][pl.ds(blocks + group * cap, cap)] = jnp.zeros(
                    (cap, length, cases), jnp.bfloat16
                )

    for b in range(blocks):
        diagonal_wide[b] = jnp.broadcast_to(
            wide[:, blocks + b : blocks + b + 1], (length, cases)
        )

    @pl.loop(0, blocks)
    def _(b):
        source = heat[b].astype(jnp.float32)
        residual[b] = source
        direction[b] = source * first_scale
        ext0[b] = first_value(b)

    first = lax.rem(me * blocks, LANES)
    aligned = pl.multiple_of(me * blocks - first, LANES)
    window = owner_map[:, pl.ds(aligned, LANES)]
    mine = window[:, :blocks]
    for start in range(blocks, LANES, blocks):
        mine = jnp.where(first == start, window[:, start : start + blocks], mine)
    down_rows = lax.broadcasted_iota(jnp.int32, (blocks, LANES), 0)
    along = lax.broadcasted_iota(jnp.int32, (blocks, LANES), 1)
    small_rows = lax.broadcasted_iota(jnp.int32, (blocks, blocks), 0)
    small_along = lax.broadcasted_iota(jnp.int32, (blocks, blocks), 1)
    away = lax.rem(mine[0:1] - me + devices, devices)
    of_slot = mine[1:2] == small_rows
    block_of = jnp.sum(jnp.where(of_slot, small_along, 0), axis=1, keepdims=True)
    distance = jnp.sum(jnp.where(of_slot, away, 0), axis=1, keepdims=True)
    distance_row = jnp.sum(
        jnp.where(small_rows == small_along, distance, 0), axis=0, keepdims=True
    )
    before = jnp.logical_and(distance == distance_row, small_along < small_rows)
    rank = jnp.sum(jnp.where(before, 1, 0), axis=1, keepdims=True)
    target_place = lax.rem(me + distance, devices) * share + rank
    source_place = lax.rem(me - distance + devices, devices) * share + rank
    table_rows[...] = jnp.zeros(table_rows.shape, jnp.int32)
    sent = jnp.sum(jnp.where(target_place == along, block_of, 0), axis=0, keepdims=True)
    held = jnp.sum(jnp.where(down_rows == along, source_place, 0), axis=0, keepdims=True)
    table_rows[0:1] = jnp.clip(sent, 0, blocks - 1)
    table_rows[1:2] = jnp.clip(held, 0, places - 1)
    table_copy = pltpu.make_async_copy(table_rows, table, table_sem)
    table_copy.start()

    field_copy = pltpu.make_async_copy(displacement, brick_field, heat_sem)
    field_copy.start()
    tile_copy.wait()

    for it in range(ITERS):
        ext = exts[it]
        old_weight, res_weight = weights[it]
        last = it == ITERS - 1

        @pl.loop(0, blocks)
        def _(b):
            own = jnp.dot(tiles[b, 0], ext[b], preferred_element_type=jnp.float32)
            held = direction[b]
            left = (
                residual[b] - diagonal_wide[b] * held - active_wide[b].astype(jnp.float32) * own
            )
            mixed = old_weight * held + res_weight * left
            summed = held if it == 0 else total[b] + held
            if last:
                total[b] = summed + mixed
            else:
                residual[b] = left
                direction[b] = mixed
                total[b] = summed

        for group, step in enumerate(GHOST_STEPS):

            @pl.when(inside(me - step))
            def _():
                for part in range(PIECES):
                    ghost_copy(it, group, part).wait_recv()

        def far_of(b):
            chosen = [ext[blocks + b]]
            for k in range(2, tile_count):
                chosen.append(ext[pattern[k, b]])
            line = jnp.concatenate([tiles[b, k] for k in range(1, tile_count)], axis=1)
            far = jnp.dot(line, jnp.concatenate(chosen, axis=0), preferred_element_type=jnp.float32)
            return active_wide[b].astype(jnp.float32) * far

        if last:
            break
        if it > 0:
            wait_sent(it - 1)

        def next_value(b):
            value = direction[b] - res_weight * far_of(b)
            return (value * active_wide[b].astype(jnp.float32)).astype(jnp.bfloat16)

        send_ghosts(it + 1, next_value)

        @pl.loop(0, blocks, unroll=2)
        def _(b):
            far = far_of(b)
            residual[b] = residual[b] - far
            held = direction[b] - res_weight * far
            direction[b] = held
            exts[it + 1][b] = (held * active_wide[b].astype(jnp.float32)).astype(jnp.bfloat16)

    unit = length // sum(Z_SHARES)
    starts = [unit * sum(Z_SHARES[:c]) for c in range(Z_CHUNKS + 1)]
    spare = ITERS % 2 * ghosts

    def levels(c):
        return pl.ds(starts[c], starts[c + 1] - starts[c])

    def brick_copy(c, target, source):
        return pltpu.make_async_remote_copy(
            src_ref=outgoing.at[pl.ds(spare + target * share, share), levels(c)],
            dst_ref=arrived[c].at[pl.ds(source * share, share)],
            send_sem=out_sem.at[c, target],
            recv_sem=in_sem.at[c, source],
            device_id=place(target),
            device_id_type=MESH,
        )

    wait_sent(ITERS - 2)
    table_copy.wait()

    def final(b):
        return (total[b] - res_weight * far_of(b)).astype(jnp.bfloat16)

    @pl.loop(1, devices)
    def _(i):
        target = lax.rem(me + i, devices)
        for r in range(share):
            outgoing[spare + target * share + r] = final(table[0, target * share + r])
        brick_copy(0, target, me).start()

    for r in range(share):
        value = final(table[0, me * share + r])
        for c in range(Z_CHUNKS):
            arrived[c][me * share + r] = value[starts[c] : starts[c + 1]]

    nx = blocks // ny
    span = nx + 2
    field, dilated, held_bricks, part, live = ext0, ext1, bricks, residual, tiles
    scale = ALPHA_T * 0.5

    def at(x, y):
        return (y + 1) * span + x + 1

    beside = (
        (col + 1 < cols, (row, col + 1)),
        (col > 0, (row, col - 1)),
        (row + 1 < rows, (row + 1, col)),
        (row > 0, (row - 1, col)),
    )
    behind = (1, 0, 3, 2)

    def halo_copies(buffer, turn, c, way):
        def copy(source, target, size, sem):
            return pltpu.make_async_remote_copy(
                src_ref=buffer.at[pl.ds(source, size), levels(c)],
                dst_ref=buffer.at[pl.ds(target, size), levels(c)],
                send_sem=sem.at[0],
                recv_sem=sem.at[1],
                device_id=beside[way][1],
                device_id_type=MESH,
            )

        if way == 0:
            return [copy(at(0, ny - 1), at(0, -1), nx, sem_y.at[turn, c, way])]
        if way == 1:
            return [copy(at(0, 0), at(0, ny), nx, sem_y.at[turn, c, way])]
        if way == 2:
            ends = (nx - 1, -1)
        else:
            ends = (0, nx)
        return [
            copy(at(ends[0], y), at(ends[1], y), 1, sem_x.at[turn, c, way - 2, y])
            for y in range(ny)
        ]

    def send_halo(buffer, turn, c, way):
        @pl.when(beside[way][0])
        def _():
            for copy in halo_copies(buffer, turn, c, way):
                copy.start()

    def wait_halo(buffer, turn, c, way):
        @pl.when(beside[behind[way]][0])
        def _():
            for copy in halo_copies(buffer, turn, c, way):
                copy.wait_recv()

    for buffer in (field, dilated):
        for way, start, size in ((0, at(0, -1), nx), (1, at(0, ny), nx)):

            @pl.when(jnp.logical_not(beside[behind[way]][0]))
            def _():
                buffer[pl.ds(start, size)] = jnp.zeros((size, length, cases), jnp.bfloat16)

        for way, x in ((2, -1), (3, nx)):

            @pl.when(jnp.logical_not(beside[behind[way]][0]))
            def _():
                for y in range(ny):
                    buffer[at(x, y)] = jnp.zeros((length, cases), jnp.bfloat16)

    for half in range(3):
        flags = bonds[pl.ds(half * 2 * blocks, 2 * blocks)].astype(jnp.float32).T
        for j in range(2 * blocks):
            live[j % blocks, half * 2 + j // blocks] = jnp.broadcast_to(
                flags[:, j : j + 1], (length, cases)
            ).astype(jnp.bfloat16)

    field_copy.wait()

    def edges(body, ready):
        @pl.loop(0, nx, unroll=2)
        def _(x):
            body(x, 0)
            body(x, ny - 1)

        ready(0)
        ready(1)
        for y in range(1, ny - 1):
            body(0, y)
            body(nx - 1, y)

        ready(2)
        ready(3)

    def inside_cells(body):
        @pl.loop(1, nx - 1, unroll=2)
        def _(x):
            for y in range(1, ny - 1):
                body(x, y)

    def receive(c):
        def cell(x, y):
            b = x * ny + y
            value = arrived[c][table[1, b]]
            held_bricks[b, levels(c)] = value
            moving = brick_field[b, levels(c)].astype(jnp.float32)
            field[at(x, y), levels(c)] = (moving - scale * value.astype(jnp.float32)).astype(
                jnp.bfloat16
            )

        edges(cell, lambda way: send_halo(field, 0, c, way))
        inside_cells(cell)

    def stencil(buffer, c, x, y):
        low = max(starts[c] - ROW_TILE, 0)
        high = min(starts[c + 1] + ROW_TILE, length)
        inner = slice(starts[c] - low, starts[c + 1] - low)
        b = x * ny + y
        centre = buffer[at(x, y), pl.ds(low, high - low)].astype(jnp.float32)
        terms = (
            (2, pltpu.roll(centre, high - low - 1, 0)[inner]),
            (5, pltpu.roll(centre, 1, 0)[inner]),
            (0, buffer[at(x + 1, y), levels(c)].astype(jnp.float32)),
            (3, buffer[at(x - 1, y), levels(c)].astype(jnp.float32)),
            (1, buffer[at(x, y + 1), levels(c)].astype(jnp.float32)),
            (4, buffer[at(x, y - 1), levels(c)].astype(jnp.float32)),
        )
        summed = count = None
        for d, value in terms:
            bond = live[b, d, levels(c)].astype(jnp.float32)
            summed = bond * value if summed is None else summed + bond * value
            count = bond if count is None else count + bond
        return summed, count

    def dilate(c):
        def cell(x, y):
            b = x * ny + y
            summed, count = stencil(field, c, x, y)
            moving = brick_field[b, levels(c)].astype(jnp.float32)
            warm = scale * held_bricks[b, levels(c)].astype(jnp.float32)
            value = (summed - count * (moving + warm)) * (1.0 / 6.0)
            part[b, levels(c)] = value
            dilated[at(x, y), levels(c)] = value.astype(jnp.bfloat16)

        if c == Z_CHUNKS - 1:
            inside_cells(cell)
        for way in range(4):
            wait_halo(field, 0, c, way)
        edges(cell, lambda way: send_halo(dilated, 1, c, way))
        if c < Z_CHUNKS - 1:
            inside_cells(cell)

    def move(c):
        def cell(x, y):
            b = x * ny + y
            summed, count = stencil(dilated, c, x, y)
            centre = part[b, levels(c)]
            force = BOND_STIFFNESS * 6.0 * centre + STATE_STIFFNESS * (summed - count * centre)
            moving = brick_field[b, levels(c)].astype(jnp.float32)
            brick_field[b, levels(c)] = (moving + STEP_SIZE * force).astype(jnp.bfloat16)

        inside_cells(cell)
        for way in range(4):
            wait_halo(dilated, 1, c, way)
        edges(cell, lambda way: None)

    for step in range(Z_CHUNKS + 2):
        if step < Z_CHUNKS:

            @pl.loop(1, devices)
            def _(i):
                target = lax.rem(me + i, devices)
                brick_copy(step, target, me).wait_send()
                if step + 1 < Z_CHUNKS:
                    brick_copy(step + 1, target, me).start()

            @pl.loop(1, devices)
            def _(i):
                brick_copy(step, me, lax.rem(me + devices - i, devices)).wait_recv()

            receive(step)
        if 1 <= step <= Z_CHUNKS:
            dilate(step - 1)
        if step >= 2:
            move(step - 2)

    wait_sent(ITERS - 1)

    for turn, buffer in enumerate((field, dilated)):
        for c in range(Z_CHUNKS):
            for way in range(4):

                @pl.when(beside[way][0])
                def _():
                    for copy in halo_copies(buffer, turn, c, way):
                        copy.wait_send()


def fused(pattern, send_list, owner_map, heat, active, diagonal, conductance, displacement, bonds, devices, ny):
    blocks, length, cases = heat.shape
    ghosts = send_list.shape[1] * send_list.shape[2]
    places = devices * max(1, blocks // devices)
    smem = pl.BlockSpec(memory_space=pltpu.SMEM)
    vmem = pl.BlockSpec(memory_space=pltpu.VMEM)
    hbm = pl.BlockSpec(memory_space=pl.ANY)
    state = pltpu.VMEM((blocks, length, cases), jnp.float32)
    ext = pltpu.VMEM((max(blocks + ghosts, (blocks // ny + 2) * (ny + 2)), length, cases), jnp.bfloat16)
    half = pltpu.VMEM((blocks, length, cases), jnp.bfloat16)
    dma = pltpu.SemaphoreType.DMA
    result = pltpu.VMEM((blocks, length, cases), jnp.bfloat16)
    return pl.pallas_call(
        functools.partial(fused_kernel, ny),
        out_shape=(result, result),
        in_specs=[smem, smem, vmem, hbm, vmem, vmem, hbm, hbm, vmem],
        out_specs=(vmem, vmem),
        scratch_shapes=[
            pltpu.VMEM(conductance.shape, jnp.bfloat16),
            ext,
            ext,
            ext,
            pltpu.VMEM((ghosts + max(ghosts, places), length, cases), jnp.bfloat16),
            state,
            state,
            state,
            half,
            state,
            pltpu.VMEM((8, LANES), jnp.int32),
            pltpu.SMEM((8, LANES), jnp.int32),
            *[
                pltpu.VMEM((places, length // sum(Z_SHARES) * share, cases), jnp.bfloat16)
                for share in Z_SHARES
            ],
            dma,
            dma,
            dma,
            dma((ITERS, len(GHOST_STEPS), PIECES)),
            dma((ITERS, len(GHOST_STEPS), PIECES)),
            dma((Z_CHUNKS, devices)),
            dma((Z_CHUNKS, devices)),
            dma((2, Z_CHUNKS, 2, 2)),
            dma((2, Z_CHUNKS, 2, ny, 2)),
        ],
        compiler_params=pltpu.CompilerParams(
            collective_id=0, has_side_effects=True, vmem_limit_bytes=57 * MIB
        ),
        name="fused",
    )(pattern, send_list, owner_map, heat, active, diagonal, conductance, displacement, bonds)


def settle_kernel(bricks, moved, bricks_out, moved_out, sems):
    copies = []
    for i, (source, target) in enumerate(((bricks, bricks_out), (moved, moved_out))):
        half = source.shape[0] // 2
        for j in range(2):
            part = pl.ds(j * half, half)
            copies.append(
                pltpu.make_async_copy(source.at[part], target.at[part], sems.at[i, j])
            )
    for copy in copies:
        copy.start()
    for copy in copies:
        copy.wait()


def settle(bricks, moved):
    vmem = pl.BlockSpec(memory_space=pltpu.VMEM)
    hbm = pl.BlockSpec(memory_space=pl.ANY)
    result = jax.ShapeDtypeStruct(bricks.shape, bricks.dtype)
    return pl.pallas_call(
        settle_kernel,
        out_shape=(result, result),
        in_specs=[vmem, vmem],
        out_specs=(hbm, hbm),
        scratch_shapes=[pltpu.SemaphoreType.DMA((2, 2))],
        compiler_params=pltpu.CompilerParams(vmem_limit_bytes=8 * MIB),
        name="settle",
    )(bricks, moved)


def local(
    heat_source,
    diagonal,
    active,
    conductance,
    pattern,
    send_list,
    owner_map,
    displacement,
    bond_live,
):
    blocks, tile_count, length = conductance.shape[:3]
    cases = heat_source.shape[1]
    devices = lax.axis_size(("row", "col"))

    bricks, moved = fused(
        pattern.T,
        send_list,
        owner_map,
        heat_source.reshape(blocks, length, cases),
        active.reshape(blocks, length),
        diagonal.reshape(blocks, length),
        conductance,
        displacement.reshape(blocks, length, cases),
        bond_live.reshape(-1, length),
        devices,
        displacement.shape[1],
    )
    bricks, moved = settle(
        bricks,
        moved,
    )
    return (bricks.reshape(displacement.shape), moved.reshape(displacement.shape))


def solution(mesh):
    return jax.shard_map(
        local,
        mesh=mesh,
        in_specs=(
            P(("row", "col"), None),
            P(("row", "col")),
            P(("row", "col")),
            P(("row", "col"), None, None, None),
            P(("row", "col"), None),
            P(("row", "col"), None, None),
            P(),
            P("row", "col", None, None),
            P(None, "row", "col", None),
        ),
        out_specs=(P("row", "col", None, None), P("row", "col", None, None)),
        check_vma=False,
    )
```

```python
import functools

import jax
import jax.numpy as jnp
from jax import lax
from jax.experimental import pallas as pl
from jax.experimental.pallas import tpu as pltpu
from jax.sharding import PartitionSpec as P

ITERS = 3
LOWER = 1.0
UPPER = 10.0
ALPHA_T = 0.5
BOND_STIFFNESS = 1.0
STATE_STIFFNESS = 2.0
STEP_SIZE = 0.1
GHOST_STEPS = (1, -1, 2, -2)
SEND_ORDER = (2, 3, 0, 1)
Z_SHARES = (2, 2, 2, 2)
Z_CHUNKS = len(Z_SHARES)
PIECES = 2
LANES = 128
ROW_TILE = 16
MESH = pl.DeviceIdType.MESH
MIB = 1024 * 1024


def chebyshev_weights(count):
    center = (UPPER + LOWER) / 2.0
    half_width = (UPPER - LOWER) / 2.0
    ratio_value = center / half_width
    previous = 1.0 / ratio_value
    weights = []
    for step_number in range(count):
        current = 1.0 / (2.0 * ratio_value - previous)
        weights.append((current * previous, 2.0 * current / half_width))
        previous = current
    return (1.0 / center, weights)


def fused_kernel(
    ny,
    pattern,
    send_list,
    owner_map,
    heat_hbm,
    active,
    diagonal,
    conductance,
    displacement,
    bonds,
    bricks,
    moved,
    tiles,
    ext0,
    ext1,
    ext2,
    outgoing,
    residual,
    direction,
    total,
    active_wide,
    diagonal_wide,
    table_rows,
    table,
    *rest,
):
    arrived = rest[:Z_CHUNKS]
    (
        tile_sem,
        heat_sem,
        table_sem,
        send_sem,
        recv_sem,
        out_sem,
        in_sem,
        sem_y,
        sem_x,
    ) = rest[Z_CHUNKS:]
    rows, cols = lax.axis_size("row"), lax.axis_size("col")
    devices = rows * cols
    row, col = lax.axis_index("row"), lax.axis_index("col")
    me = row * cols + col
    brick_field = moved
    blocks, length, cases = brick_field.shape
    tile_count = tiles.shape[1]
    cap = send_list.shape[2]
    ghosts = cap * len(GHOST_STEPS)
    places = arrived[0].shape[0]
    share = places // devices
    exts = (ext0, ext1, ext2)
    first_scale, weights = chebyshev_weights(ITERS)

    heat = brick_field
    heat_copy = pltpu.make_async_copy(heat_hbm, heat, heat_sem)
    heat_copy.start()
    tile_copy = pltpu.make_async_copy(conductance, tiles, tile_sem)

    def inside(index):
        return jnp.logical_and(index >= 0, index < devices)

    def place(index):
        return (lax.div(index, cols), lax.rem(index, cols))

    barrier = pltpu.get_barrier_semaphore()

    @pl.loop(1, devices)
    def _(i):
        peer = lax.rem(me + i, devices)
        pl.semaphore_signal(barrier, inc=1, device_id=place(peer), device_id_type=MESH)

    piece = cap // PIECES

    def ghost_copy(it, group, part):
        first = group * cap + part * piece
        return pltpu.make_async_remote_copy(
            src_ref=outgoing.at[pl.ds((it % 2) * ghosts + first, piece)],
            dst_ref=exts[it].at[pl.ds(blocks + first, piece)],
            send_sem=send_sem.at[it, group, part],
            recv_sem=recv_sem.at[it, group, part],
            device_id=place(me + GHOST_STEPS[group]),
            device_id_type=MESH,
        )

    wide = jnp.concatenate([active[...].astype(jnp.float32), diagonal[...]], axis=0).T
    for b in range(blocks):
        column = jnp.broadcast_to(wide[:, b : b + 1], (length, cases))
        active_wide[b] = column.astype(jnp.bfloat16)

    heat_copy.wait()

    def first_value(b):
        start = heat[b].astype(jnp.float32) * first_scale
        return (start * active_wide[b].astype(jnp.float32)).astype(jnp.bfloat16)

    def wait_sent(it):
        for group, step in enumerate(GHOST_STEPS):

            @pl.when(inside(me + step))
            def _():
                for part in range(PIECES):
                    ghost_copy(it, group, part).wait_send()

    def send_ghosts(it, value_of):
        @pl.loop(0, PIECES)
        def _(part):
            for group in SEND_ORDER:
                for i in range(piece):
                    j = part * piece + i
                    outgoing[it % 2 * ghosts + group * cap + j] = value_of(send_list[0, group, j])

                @pl.when(inside(me + GHOST_STEPS[group]))
                def _():
                    ghost_copy(it, group, part).start()

    pl.semaphore_wait(barrier, devices - 1)
    send_ghosts(0, first_value)
    tile_copy.start()

    for it in range(ITERS):
        for group, step in enumerate(GHOST_STEPS):

            @pl.when(jnp.logical_not(inside(me - step)))
            def _():
                exts[it][pl.ds(blocks + group * cap, cap)] = jnp.zeros(
                    (cap, length, cases), jnp.bfloat16
                )

    for b in range(blocks):
        diagonal_wide[b] = jnp.broadcast_to(
            wide[:, blocks + b : blocks + b + 1], (length, cases)
        )

    @pl.loop(0, blocks)
    def _(b):
        source = heat[b].astype(jnp.float32)
        residual[b] = source
        direction[b] = source * first_scale
        ext0[b] = first_value(b)

    first = lax.rem(me * blocks, LANES)
    aligned = pl.multiple_of(me * blocks - first, LANES)
    window = owner_map[:, pl.ds(aligned, LANES)]
    mine = window[:, :blocks]
    for start in range(blocks, LANES, blocks):
        mine = jnp.where(first == start, window[:, start : start + blocks], mine)
    down_rows = lax.broadcasted_iota(jnp.int32, (blocks, LANES), 0)
    along = lax.broadcasted_iota(jnp.int32, (blocks, LANES), 1)
    small_rows = lax.broadcasted_iota(jnp.int32, (blocks, blocks), 0)
    small_along = lax.broadcasted_iota(jnp.int32, (blocks, blocks), 1)
    away = lax.rem(mine[0:1] - me + devices, devices)
    of_slot = mine[1:2] == small_rows
    block_of = jnp.sum(jnp.where(of_slot, small_along, 0), axis=1, keepdims=True)
    distance = jnp.sum(jnp.where(of_slot, away, 0), axis=1, keepdims=True)
    distance_row = jnp.sum(
        jnp.where(small_rows == small_along, distance, 0), axis=0, keepdims=True
    )
    before = jnp.logical_and(distance == distance_row, small_along < small_rows)
    rank = jnp.sum(jnp.where(before, 1, 0), axis=1, keepdims=True)
    target_place = lax.rem(me + distance, devices) * share + rank
    source_place = lax.rem(me - distance + devices, devices) * share + rank
    table_rows[...] = jnp.zeros(table_rows.shape, jnp.int32)
    sent = jnp.sum(jnp.where(target_place == along, block_of, 0), axis=0, keepdims=True)
    held = jnp.sum(jnp.where(down_rows == along, source_place, 0), axis=0, keepdims=True)
    table_rows[0:1] = jnp.clip(sent, 0, blocks - 1)
    table_rows[1:2] = jnp.clip(held, 0, places - 1)
    table_copy = pltpu.make_async_copy(table_rows, table, table_sem)
    table_copy.start()

    field_copy = pltpu.make_async_copy(displacement, brick_field, heat_sem)
    field_copy.start()
    tile_copy.wait()

    for it in range(ITERS):
        ext = exts[it]
        old_weight, res_weight = weights[it]
        last = it == ITERS - 1

        @pl.loop(0, blocks)
        def _(b):
            own = jnp.dot(tiles[b, 0], ext[b], preferred_element_type=jnp.float32)
            held = direction[b]
            left = (
                residual[b] - diagonal_wide[b] * held - active_wide[b].astype(jnp.float32) * own
            )
            mixed = old_weight * held + res_weight * left
            summed = held if it == 0 else total[b] + held
            if last:
                total[b] = summed + mixed
            else:
                residual[b] = left
                direction[b] = mixed
                total[b] = summed

        for group, step in enumerate(GHOST_STEPS):

            @pl.when(inside(me - step))
            def _():
                for part in range(PIECES):
                    ghost_copy(it, group, part).wait_recv()

        def far_of(b):
            chosen = [ext[blocks + b]]
            for k in range(2, tile_count):
                chosen.append(ext[pattern[k, b]])
            line = jnp.concatenate([tiles[b, k] for k in range(1, tile_count)], axis=1)
            far = jnp.dot(line, jnp.concatenate(chosen, axis=0), preferred_element_type=jnp.float32)
            return active_wide[b].astype(jnp.float32) * far

        if last:
            break
        if it > 0:
            wait_sent(it - 1)

        def next_value(b):
            value = direction[b] - res_weight * far_of(b)
            return (value * active_wide[b].astype(jnp.float32)).astype(jnp.bfloat16)

        send_ghosts(it + 1, next_value)

        @pl.loop(0, blocks, unroll=2)
        def _(b):
            far = far_of(b)
            residual[b] = residual[b] - far
            held = direction[b] - res_weight * far
            direction[b] = held
            exts[it + 1][b] = (held * active_wide[b].astype(jnp.float32)).astype(jnp.bfloat16)

    unit = length // sum(Z_SHARES)
    starts = [unit * sum(Z_SHARES[:c]) for c in range(Z_CHUNKS + 1)]
    spare = ITERS % 2 * ghosts

    def levels(c):
        return pl.ds(starts[c], starts[c + 1] - starts[c])

    def brick_copy(c, target, source):
        return pltpu.make_async_remote_copy(
            src_ref=outgoing.at[pl.ds(spare + target * share, share), levels(c)],
            dst_ref=arrived[c].at[pl.ds(source * share, share)],
            send_sem=out_sem.at[c, target],
            recv_sem=in_sem.at[c, source],
            device_id=place(target),
            device_id_type=MESH,
        )

    wait_sent(ITERS - 2)
    table_copy.wait()

    def final(b):
        return (total[b] - res_weight * far_of(b)).astype(jnp.bfloat16)

    @pl.loop(1, devices)
    def _(i):
        target = lax.rem(me + i, devices)
        for r in range(share):
            outgoing[spare + target * share + r] = final(table[0, target * share + r])
        brick_copy(0, target, me).start()

    for r in range(share):
        value = final(table[0, me * share + r])
        for c in range(Z_CHUNKS):
            arrived[c][me * share + r] = value[starts[c] : starts[c + 1]]

    nx = blocks // ny
    span = nx + 2
    field, dilated, held_bricks, part, live = ext0, ext1, bricks, residual, tiles
    scale = ALPHA_T * 0.5

    def at(x, y):
        return (y + 1) * span + x + 1

    beside = (
        (col + 1 < cols, (row, col + 1)),
        (col > 0, (row, col - 1)),
        (row + 1 < rows, (row + 1, col)),
        (row > 0, (row - 1, col)),
    )
    behind = (1, 0, 3, 2)

    def halo_copies(buffer, turn, c, way):
        def copy(source, target, size, sem):
            return pltpu.make_async_remote_copy(
                src_ref=buffer.at[pl.ds(source, size), levels(c)],
                dst_ref=buffer.at[pl.ds(target, size), levels(c)],
                send_sem=sem.at[0],
                recv_sem=sem.at[1],
                device_id=beside[way][1],
                device_id_type=MESH,
            )

        if way == 0:
            return [copy(at(0, ny - 1), at(0, -1), nx, sem_y.at[turn, c, way])]
        if way == 1:
            return [copy(at(0, 0), at(0, ny), nx, sem_y.at[turn, c, way])]
        if way == 2:
            ends = (nx - 1, -1)
        else:
            ends = (0, nx)
        return [
            copy(at(ends[0], y), at(ends[1], y), 1, sem_x.at[turn, c, way - 2, y])
            for y in range(ny)
        ]

    def send_halo(buffer, turn, c, way):
        @pl.when(beside[way][0])
        def _():
            for copy in halo_copies(buffer, turn, c, way):
                copy.start()

    def wait_halo(buffer, turn, c, way):
        @pl.when(beside[behind[way]][0])
        def _():
            for copy in halo_copies(buffer, turn, c, way):
                copy.wait_recv()

    for buffer in (field, dilated):
        for way, start, size in ((0, at(0, -1), nx), (1, at(0, ny), nx)):

            @pl.when(jnp.logical_not(beside[behind[way]][0]))
            def _():
                buffer[pl.ds(start, size)] = jnp.zeros((size, length, cases), jnp.bfloat16)

        for way, x in ((2, -1), (3, nx)):

            @pl.when(jnp.logical_not(beside[behind[way]][0]))
            def _():
                for y in range(ny):
                    buffer[at(x, y)] = jnp.zeros((length, cases), jnp.bfloat16)

    for half in range(3):
        flags = bonds[pl.ds(half * 2 * blocks, 2 * blocks)].astype(jnp.float32).T
        for j in range(2 * blocks):
            live[j % blocks, half * 2 + j // blocks] = jnp.broadcast_to(
                flags[:, j : j + 1], (length, cases)
            ).astype(jnp.bfloat16)

    field_copy.wait()

    def edges(body, ready):
        @pl.loop(0, nx, unroll=2)
        def _(x):
            body(x, 0)
            body(x, ny - 1)

        ready(0)
        ready(1)
        for y in range(1, ny - 1):
            body(0, y)
            body(nx - 1, y)

        ready(2)
        ready(3)

    def inside_cells(body):
        @pl.loop(1, nx - 1, unroll=2)
        def _(x):
            for y in range(1, ny - 1):
                body(x, y)

    def receive(c):
        def cell(x, y):
            b = x * ny + y
            value = arrived[c][table[1, b]]
            held_bricks[b, levels(c)] = value
            moving = brick_field[b, levels(c)].astype(jnp.float32)
            field[at(x, y), levels(c)] = (moving - scale * value.astype(jnp.float32)).astype(
                jnp.bfloat16
            )

        edges(cell, lambda way: send_halo(field, 0, c, way))
        inside_cells(cell)

    def stencil(buffer, c, x, y):
        low = max(starts[c] - ROW_TILE, 0)
        high = min(starts[c + 1] + ROW_TILE, length)
        inner = slice(starts[c] - low, starts[c + 1] - low)
        b = x * ny + y
        centre = buffer[at(x, y), pl.ds(low, high - low)].astype(jnp.float32)
        terms = (
            (2, pltpu.roll(centre, high - low - 1, 0)[inner]),
            (5, pltpu.roll(centre, 1, 0)[inner]),
            (0, buffer[at(x + 1, y), levels(c)].astype(jnp.float32)),
            (3, buffer[at(x - 1, y), levels(c)].astype(jnp.float32)),
            (1, buffer[at(x, y + 1), levels(c)].astype(jnp.float32)),
            (4, buffer[at(x, y - 1), levels(c)].astype(jnp.float32)),
        )
        summed = count = None
        for d, value in terms:
            bond = live[b, d, levels(c)].astype(jnp.float32)
            summed = bond * value if summed is None else summed + bond * value
            count = bond if count is None else count + bond
        return summed, count

    def dilate(c):
        def cell(x, y):
            b = x * ny + y
            summed, count = stencil(field, c, x, y)
            moving = brick_field[b, levels(c)].astype(jnp.float32)
            warm = scale * held_bricks[b, levels(c)].astype(jnp.float32)
            value = (summed - count * (moving + warm)) * (1.0 / 6.0)
            part[b, levels(c)] = value
            dilated[at(x, y), levels(c)] = value.astype(jnp.bfloat16)

        if c == Z_CHUNKS - 1:
            inside_cells(cell)
        for way in range(4):
            wait_halo(field, 0, c, way)
        edges(cell, lambda way: send_halo(dilated, 1, c, way))
        if c < Z_CHUNKS - 1:
            inside_cells(cell)

    def move(c):
        def cell(x, y):
            b = x * ny + y
            summed, count = stencil(dilated, c, x, y)
            centre = part[b, levels(c)]
            force = BOND_STIFFNESS * 6.0 * centre + STATE_STIFFNESS * (summed - count * centre)
            moving = brick_field[b, levels(c)].astype(jnp.float32)
            brick_field[b, levels(c)] = (moving + STEP_SIZE * force).astype(jnp.bfloat16)

        inside_cells(cell)
        for way in range(4):
            wait_halo(dilated, 1, c, way)
        edges(cell, lambda way: None)

    for step in range(Z_CHUNKS + 2):
        if step < Z_CHUNKS:

            @pl.loop(1, devices)
            def _(i):
                target = lax.rem(me + i, devices)
                brick_copy(step, target, me).wait_send()
                if step + 1 < Z_CHUNKS:
                    brick_copy(step + 1, target, me).start()

            @pl.loop(1, devices)
            def _(i):
                brick_copy(step, me, lax.rem(me + devices - i, devices)).wait_recv()

            receive(step)
        if 1 <= step <= Z_CHUNKS:
            dilate(step - 1)
        if step >= 2:
            move(step - 2)

    wait_sent(ITERS - 1)

    for turn, buffer in enumerate((field, dilated)):
        for c in range(Z_CHUNKS):
            for way in range(4):

                @pl.when(beside[way][0])
                def _():
                    for copy in halo_copies(buffer, turn, c, way):
                        copy.wait_send()


def fused(pattern, send_list, owner_map, heat, active, diagonal, conductance, displacement, bonds, devices, ny):
    blocks, length, cases = heat.shape
    ghosts = send_list.shape[1] * send_list.shape[2]
    places = devices * max(1, blocks // devices)
    smem = pl.BlockSpec(memory_space=pltpu.SMEM)
    vmem = pl.BlockSpec(memory_space=pltpu.VMEM)
    hbm = pl.BlockSpec(memory_space=pl.ANY)
    state = pltpu.VMEM((blocks, length, cases), jnp.float32)
    ext = pltpu.VMEM((max(blocks + ghosts, (blocks // ny + 2) * (ny + 2)), length, cases), jnp.bfloat16)
    half = pltpu.VMEM((blocks, length, cases), jnp.bfloat16)
    dma = pltpu.SemaphoreType.DMA
    result = pltpu.VMEM((blocks, length, cases), jnp.bfloat16)
    return pl.pallas_call(
        functools.partial(fused_kernel, ny),
        out_shape=(result, result),
        in_specs=[smem, smem, vmem, hbm, vmem, vmem, hbm, hbm, vmem],
        out_specs=(vmem, vmem),
        scratch_shapes=[
            pltpu.VMEM(conductance.shape, jnp.bfloat16),
            ext,
            ext,
            ext,
            pltpu.VMEM((ghosts + max(ghosts, places), length, cases), jnp.bfloat16),
            state,
            state,
            state,
            half,
            state,
            pltpu.VMEM((8, LANES), jnp.int32),
            pltpu.SMEM((8, LANES), jnp.int32),
            *[
                pltpu.VMEM((places, length // sum(Z_SHARES) * share, cases), jnp.bfloat16)
                for share in Z_SHARES
            ],
            dma,
            dma,
            dma,
            dma((ITERS, len(GHOST_STEPS), PIECES)),
            dma((ITERS, len(GHOST_STEPS), PIECES)),
            dma((Z_CHUNKS, devices)),
            dma((Z_CHUNKS, devices)),
            dma((2, Z_CHUNKS, 2, 2)),
            dma((2, Z_CHUNKS, 2, ny, 2)),
        ],
        compiler_params=pltpu.CompilerParams(
            collective_id=0, has_side_effects=True, vmem_limit_bytes=57 * MIB
        ),
        name="fused",
    )(pattern, send_list, owner_map, heat, active, diagonal, conductance, displacement, bonds)


def settle_kernel(bricks, moved, bricks_out, moved_out, sems):
    copies = []
    for i, (source, target) in enumerate(((bricks, bricks_out), (moved, moved_out))):
        half = source.shape[0] // 2
        for j in range(2):
            part = pl.ds(j * half, half)
            copies.append(
                pltpu.make_async_copy(source.at[part], target.at[part], sems.at[i, j])
            )
    for copy in copies:
        copy.start()
    for copy in copies:
        copy.wait()


def settle(bricks, moved):
    vmem = pl.BlockSpec(memory_space=pltpu.VMEM)
    hbm = pl.BlockSpec(memory_space=pl.ANY)
    result = jax.ShapeDtypeStruct(bricks.shape, bricks.dtype)
    return pl.pallas_call(
        settle_kernel,
        out_shape=(result, result),
        in_specs=[vmem, vmem],
        out_specs=(hbm, hbm),
        scratch_shapes=[pltpu.SemaphoreType.DMA((2, 2))],
        compiler_params=pltpu.CompilerParams(vmem_limit_bytes=8 * MIB),
        name="settle",
    )(bricks, moved)


def local(
    heat_source,
    diagonal,
    active,
    conductance,
    pattern,
    send_list,
    owner_map,
    displacement,
    bond_live,
):
    blocks, tile_count, length = conductance.shape[:3]
    cases = heat_source.shape[1]
    devices = lax.axis_size(("row", "col"))

    bricks, moved = fused(
        pattern.T,
        send_list,
        owner_map,
        heat_source.reshape(blocks, length, cases),
        active.reshape(blocks, length),
        diagonal.reshape(blocks, length),
        conductance,
        displacement.reshape(blocks, length, cases),
        bond_live.reshape(-1, length),
        devices,
        displacement.shape[1],
    )
    bricks, moved = settle(
        bricks,
        moved,
    )
    return (bricks.reshape(displacement.shape), moved.reshape(displacement.shape))


def solution(mesh):
    return jax.shard_map(
        local,
        mesh=mesh,
        in_specs=(
            P(("row", "col"), None),
            P(("row", "col")),
            P(("row", "col")),
            P(("row", "col"), None, None, None),
            P(("row", "col"), None),
            P(("row", "col"), None, None),
            P(),
            P("row", "col", None, None),
            P(None, "row", "col", None),
        ),
        out_specs=(P("row", "col", None, None), P("row", "col", None, None)),
        check_vma=False,
    )
```

```python
import functools

import jax
import jax.numpy as jnp
from jax import lax
from jax.experimental import pallas as pl
from jax.experimental.pallas import tpu as pltpu
from jax.sharding import PartitionSpec as P

ITERS = 3
LOWER = 1.0
UPPER = 10.0
ALPHA_T = 0.5
BOND_STIFFNESS = 1.0
STATE_STIFFNESS = 2.0
STEP_SIZE = 0.1
GHOST_STEPS = (1, -1, 2, -2)
SEND_ORDER = (2, 3, 0, 1)
Z_SHARES = (2, 2, 2, 2)
Z_CHUNKS = len(Z_SHARES)
PIECES = 2
LANES = 128
ROW_TILE = 16
MESH = pl.DeviceIdType.MESH
MIB = 1024 * 1024


def chebyshev_weights(count):
    center = (UPPER + LOWER) / 2.0
    half_width = (UPPER - LOWER) / 2.0
    ratio_value = center / half_width
    previous = 1.0 / ratio_value
    weights = []
    for step_number in range(count):
        current = 1.0 / (2.0 * ratio_value - previous)
        weights.append((current * previous, 2.0 * current / half_width))
        previous = current
    return (1.0 / center, weights)


def fused_kernel(
    ny,
    pattern,
    send_list,
    owner_map,
    heat_hbm,
    active,
    diagonal,
    conductance,
    displacement,
    bonds,
    bricks,
    moved,
    tiles,
    ext0,
    ext1,
    ext2,
    outgoing,
    residual,
    direction,
    total,
    active_wide,
    diagonal_wide,
    table_rows,
    table,
    *rest,
):
    arrived = rest[:Z_CHUNKS]
    (
        tile_sem,
        heat_sem,
        table_sem,
        send_sem,
        recv_sem,
        out_sem,
        in_sem,
        sem_y,
        sem_x,
    ) = rest[Z_CHUNKS:]
    rows, cols = lax.axis_size("row"), lax.axis_size("col")
    devices = rows * cols
    row, col = lax.axis_index("row"), lax.axis_index("col")
    me = row * cols + col
    brick_field = moved
    blocks, length, cases = brick_field.shape
    tile_count = tiles.shape[1]
    cap = send_list.shape[2]
    ghosts = cap * len(GHOST_STEPS)
    places = arrived[0].shape[0]
    share = places // devices
    exts = (ext0, ext1, ext2)
    first_scale, weights = chebyshev_weights(ITERS)

    heat = brick_field
    heat_copy = pltpu.make_async_copy(heat_hbm, heat, heat_sem)
    heat_copy.start()
    tile_copy = pltpu.make_async_copy(conductance, tiles, tile_sem)

    def inside(index):
        return jnp.logical_and(index >= 0, index < devices)

    def place(index):
        return (lax.div(index, cols), lax.rem(index, cols))

    barrier = pltpu.get_barrier_semaphore()

    @pl.loop(1, devices)
    def _(i):
        peer = lax.rem(me + i, devices)
        pl.semaphore_signal(barrier, inc=1, device_id=place(peer), device_id_type=MESH)

    piece = cap // PIECES

    def ghost_copy(it, group, part):
        first = group * cap + part * piece
        return pltpu.make_async_remote_copy(
            src_ref=outgoing.at[pl.ds((it % 2) * ghosts + first, piece)],
            dst_ref=exts[it].at[pl.ds(blocks + first, piece)],
            send_sem=send_sem.at[it, group, part],
            recv_sem=recv_sem.at[it, group, part],
            device_id=place(me + GHOST_STEPS[group]),
            device_id_type=MESH,
        )

    wide = jnp.concatenate([active[...].astype(jnp.float32), diagonal[...]], axis=0).T
    for b in range(blocks):
        column = jnp.broadcast_to(wide[:, b : b + 1], (length, cases))
        active_wide[b] = column.astype(jnp.bfloat16)

    heat_copy.wait()

    def first_value(b):
        start = heat[b].astype(jnp.float32) * first_scale
        return (start * active_wide[b].astype(jnp.float32)).astype(jnp.bfloat16)

    def wait_sent(it):
        for group, step in enumerate(GHOST_STEPS):

            @pl.when(inside(me + step))
            def _():
                for part in range(PIECES):
                    ghost_copy(it, group, part).wait_send()

    def send_ghosts(it, value_of):
        @pl.loop(0, PIECES)
        def _(part):
            for group in SEND_ORDER:
                for i in range(piece):
                    j = part * piece + i
                    outgoing[it % 2 * ghosts + group * cap + j] = value_of(send_list[0, group, j])

                @pl.when(inside(me + GHOST_STEPS[group]))
                def _():
                    ghost_copy(it, group, part).start()

    @pl.loop(0, cap)
    def _(j):
        for group in SEND_ORDER:
            outgoing[group * cap + j] = first_value(send_list[0, group, j])

    pl.semaphore_wait(barrier, devices - 1)
    for part in range(PIECES):
        for group in SEND_ORDER:

            @pl.when(inside(me + GHOST_STEPS[group]))
            def _():
                ghost_copy(0, group, part).start()

    tile_copy.start()

    for it in range(ITERS):
        for group, step in enumerate(GHOST_STEPS):

            @pl.when(jnp.logical_not(inside(me - step)))
            def _():
                exts[it][pl.ds(blocks + group * cap, cap)] = jnp.zeros(
                    (cap, length, cases), jnp.bfloat16
                )

    for b in range(blocks):
        diagonal_wide[b] = jnp.broadcast_to(
            wide[:, blocks + b : blocks + b + 1], (length, cases)
        )

    @pl.loop(0, blocks)
    def _(b):
        source = heat[b].astype(jnp.float32)
        residual[b] = source
        direction[b] = source * first_scale
        ext0[b] = first_value(b)

    first = lax.rem(me * blocks, LANES)
    aligned = pl.multiple_of(me * blocks - first, LANES)
    window = owner_map[:, pl.ds(aligned, LANES)]
    mine = window[:, :blocks]
    for start in range(blocks, LANES, blocks):
        mine = jnp.where(first == start, window[:, start : start + blocks], mine)
    down_rows = lax.broadcasted_iota(jnp.int32, (blocks, LANES), 0)
    along = lax.broadcasted_iota(jnp.int32, (blocks, LANES), 1)
    small_rows = lax.broadcasted_iota(jnp.int32, (blocks, blocks), 0)
    small_along = lax.broadcasted_iota(jnp.int32, (blocks, blocks), 1)
    away = lax.rem(mine[0:1] - me + devices, devices)
    of_slot = mine[1:2] == small_rows
    block_of = jnp.sum(jnp.where(of_slot, small_along, 0), axis=1, keepdims=True)
    distance = jnp.sum(jnp.where(of_slot, away, 0), axis=1, keepdims=True)
    distance_row = jnp.sum(
        jnp.where(small_rows == small_along, distance, 0), axis=0, keepdims=True
    )
    before = jnp.logical_and(distance == distance_row, small_along < small_rows)
    rank = jnp.sum(jnp.where(before, 1, 0), axis=1, keepdims=True)
    target_place = lax.rem(me + distance, devices) * share + rank
    source_place = lax.rem(me - distance + devices, devices) * share + rank
    table_rows[...] = jnp.zeros(table_rows.shape, jnp.int32)
    sent = jnp.sum(jnp.where(target_place == along, block_of, 0), axis=0, keepdims=True)
    held = jnp.sum(jnp.where(down_rows == along, source_place, 0), axis=0, keepdims=True)
    table_rows[0:1] = jnp.clip(sent, 0, blocks - 1)
    table_rows[1:2] = jnp.clip(held, 0, places - 1)
    table_copy = pltpu.make_async_copy(table_rows, table, table_sem)
    table_copy.start()

    field_copy = pltpu.make_async_copy(displacement, brick_field, heat_sem)
    field_copy.start()
    tile_copy.wait()

    for it in range(ITERS):
        ext = exts[it]
        old_weight, res_weight = weights[it]
        last = it == ITERS - 1

        @pl.loop(0, blocks)
        def _(b):
            own = jnp.dot(tiles[b, 0], ext[b], preferred_element_type=jnp.float32)
            held = direction[b]
            left = (
                residual[b] - diagonal_wide[b] * held - active_wide[b].astype(jnp.float32) * own
            )
            mixed = old_weight * held + res_weight * left
            summed = held if it == 0 else total[b] + held
            if last:
                total[b] = summed + mixed
            else:
                residual[b] = left
                direction[b] = mixed
                total[b] = summed

        for group, step in enumerate(GHOST_STEPS):

            @pl.when(inside(me - step))
            def _():
                for part in range(PIECES):
                    ghost_copy(it, group, part).wait_recv()

        def far_of(b):
            chosen = [ext[blocks + b]]
            for k in range(2, tile_count):
                chosen.append(ext[pattern[k, b]])
            line = jnp.concatenate([tiles[b, k] for k in range(1, tile_count)], axis=1)
            far = jnp.dot(line, jnp.concatenate(chosen, axis=0), preferred_element_type=jnp.float32)
            return active_wide[b].astype(jnp.float32) * far

        if last:
            break
        if it > 0:
            wait_sent(it - 1)

        def next_value(b):
            value = direction[b] - res_weight * far_of(b)
            return (value * active_wide[b].astype(jnp.float32)).astype(jnp.bfloat16)

        send_ghosts(it + 1, next_value)

        @pl.loop(0, blocks, unroll=2)
        def _(b):
            far = far_of(b)
            residual[b] = residual[b] - far
            held = direction[b] - res_weight * far
            direction[b] = held
            exts[it + 1][b] = (held * active_wide[b].astype(jnp.float32)).astype(jnp.bfloat16)

    unit = length // sum(Z_SHARES)
    starts = [unit * sum(Z_SHARES[:c]) for c in range(Z_CHUNKS + 1)]
    spare = ITERS % 2 * ghosts

    def levels(c):
        return pl.ds(starts[c], starts[c + 1] - starts[c])

    def brick_copy(c, target, source):
        return pltpu.make_async_remote_copy(
            src_ref=outgoing.at[pl.ds(spare + target * share, share), levels(c)],
            dst_ref=arrived[c].at[pl.ds(source * share, share)],
            send_sem=out_sem.at[c, target],
            recv_sem=in_sem.at[c, source],
            device_id=place(target),
            device_id_type=MESH,
        )

    wait_sent(ITERS - 2)
    table_copy.wait()

    def final(b):
        return (total[b] - res_weight * far_of(b)).astype(jnp.bfloat16)

    @pl.loop(1, devices)
    def _(i):
        target = lax.rem(me + i, devices)
        for r in range(share):
            outgoing[spare + target * share + r] = final(table[0, target * share + r])
        brick_copy(0, target, me).start()

    for r in range(share):
        value = final(table[0, me * share + r])
        for c in range(Z_CHUNKS):
            arrived[c][me * share + r] = value[starts[c] : starts[c + 1]]

    nx = blocks // ny
    span = nx + 2
    field, dilated, held_bricks, part, live = ext0, ext1, bricks, residual, tiles
    scale = ALPHA_T * 0.5

    def at(x, y):
        return (y + 1) * span + x + 1

    beside = (
        (col + 1 < cols, (row, col + 1)),
        (col > 0, (row, col - 1)),
        (row + 1 < rows, (row + 1, col)),
        (row > 0, (row - 1, col)),
    )
    behind = (1, 0, 3, 2)

    def halo_copies(buffer, turn, c, way):
        def copy(source, target, size, sem):
            return pltpu.make_async_remote_copy(
                src_ref=buffer.at[pl.ds(source, size), levels(c)],
                dst_ref=buffer.at[pl.ds(target, size), levels(c)],
                send_sem=sem.at[0],
                recv_sem=sem.at[1],
                device_id=beside[way][1],
                device_id_type=MESH,
            )

        if way == 0:
            return [copy(at(0, ny - 1), at(0, -1), nx, sem_y.at[turn, c, way])]
        if way == 1:
            return [copy(at(0, 0), at(0, ny), nx, sem_y.at[turn, c, way])]
        if way == 2:
            ends = (nx - 1, -1)
        else:
            ends = (0, nx)
        return [
            copy(at(ends[0], y), at(ends[1], y), 1, sem_x.at[turn, c, way - 2, y])
            for y in range(ny)
        ]

    def send_halo(buffer, turn, c, way):
        @pl.when(beside[way][0])
        def _():
            for copy in halo_copies(buffer, turn, c, way):
                copy.start()

    def wait_halo(buffer, turn, c, way):
        @pl.when(beside[behind[way]][0])
        def _():
            for copy in halo_copies(buffer, turn, c, way):
                copy.wait_recv()

    for buffer in (field, dilated):
        for way, start, size in ((0, at(0, -1), nx), (1, at(0, ny), nx)):

            @pl.when(jnp.logical_not(beside[behind[way]][0]))
            def _():
                buffer[pl.ds(start, size)] = jnp.zeros((size, length, cases), jnp.bfloat16)

        for way, x in ((2, -1), (3, nx)):

            @pl.when(jnp.logical_not(beside[behind[way]][0]))
            def _():
                for y in range(ny):
                    buffer[at(x, y)] = jnp.zeros((length, cases), jnp.bfloat16)

    for half in range(3):
        flags = bonds[pl.ds(half * 2 * blocks, 2 * blocks)].astype(jnp.float32).T
        for j in range(2 * blocks):
            live[j % blocks, half * 2 + j // blocks] = jnp.broadcast_to(
                flags[:, j : j + 1], (length, cases)
            ).astype(jnp.bfloat16)

    field_copy.wait()

    def edges(body, ready):
        @pl.loop(0, nx, unroll=2)
        def _(x):
            body(x, 0)
            body(x, ny - 1)

        ready(0)
        ready(1)
        for y in range(1, ny - 1):
            body(0, y)
            body(nx - 1, y)

        ready(2)
        ready(3)

    def inside_cells(body):
        @pl.loop(1, nx - 1, unroll=2)
        def _(x):
            for y in range(1, ny - 1):
                body(x, y)

    def receive(c):
        def cell(x, y):
            b = x * ny + y
            value = arrived[c][table[1, b]]
            held_bricks[b, levels(c)] = value
            moving = brick_field[b, levels(c)].astype(jnp.float32)
            field[at(x, y), levels(c)] = (moving - scale * value.astype(jnp.float32)).astype(
                jnp.bfloat16
            )

        edges(cell, lambda way: send_halo(field, 0, c, way))
        inside_cells(cell)

    def stencil(buffer, c, x, y):
        low = max(starts[c] - ROW_TILE, 0)
        high = min(starts[c + 1] + ROW_TILE, length)
        inner = slice(starts[c] - low, starts[c + 1] - low)
        b = x * ny + y
        centre = buffer[at(x, y), pl.ds(low, high - low)].astype(jnp.float32)
        terms = (
            (2, pltpu.roll(centre, high - low - 1, 0)[inner]),
            (5, pltpu.roll(centre, 1, 0)[inner]),
            (0, buffer[at(x + 1, y), levels(c)].astype(jnp.float32)),
            (3, buffer[at(x - 1, y), levels(c)].astype(jnp.float32)),
            (1, buffer[at(x, y + 1), levels(c)].astype(jnp.float32)),
            (4, buffer[at(x, y - 1), levels(c)].astype(jnp.float32)),
        )
        summed = count = None
        for d, value in terms:
            bond = live[b, d, levels(c)].astype(jnp.float32)
            summed = bond * value if summed is None else summed + bond * value
            count = bond if count is None else count + bond
        return summed, count

    def dilate(c):
        def cell(x, y):
            b = x * ny + y
            summed, count = stencil(field, c, x, y)
            moving = brick_field[b, levels(c)].astype(jnp.float32)
            warm = scale * held_bricks[b, levels(c)].astype(jnp.float32)
            value = (summed - count * (moving + warm)) * (1.0 / 6.0)
            part[b, levels(c)] = value
            dilated[at(x, y), levels(c)] = value.astype(jnp.bfloat16)

        if c == Z_CHUNKS - 1:
            inside_cells(cell)
        for way in range(4):
            wait_halo(field, 0, c, way)
        edges(cell, lambda way: send_halo(dilated, 1, c, way))
        if c < Z_CHUNKS - 1:
            inside_cells(cell)

    def move(c):
        def cell(x, y):
            b = x * ny + y
            summed, count = stencil(dilated, c, x, y)
            centre = part[b, levels(c)]
            force = BOND_STIFFNESS * 6.0 * centre + STATE_STIFFNESS * (summed - count * centre)
            moving = brick_field[b, levels(c)].astype(jnp.float32)
            brick_field[b, levels(c)] = (moving + STEP_SIZE * force).astype(jnp.bfloat16)

        inside_cells(cell)
        for way in range(4):
            wait_halo(dilated, 1, c, way)
        edges(cell, lambda way: None)

    for step in range(Z_CHUNKS + 2):
        if step < Z_CHUNKS:

            @pl.loop(1, devices)
            def _(i):
                target = lax.rem(me + i, devices)
                brick_copy(step, target, me).wait_send()
                if step + 1 < Z_CHUNKS:
                    brick_copy(step + 1, target, me).start()

            @pl.loop(1, devices)
            def _(i):
                brick_copy(step, me, lax.rem(me + devices - i, devices)).wait_recv()

            receive(step)
        if 1 <= step <= Z_CHUNKS:
            dilate(step - 1)
        if step >= 2:
            move(step - 2)

    wait_sent(ITERS - 1)

    for turn, buffer in enumerate((field, dilated)):
        for c in range(Z_CHUNKS):
            for way in range(4):

                @pl.when(beside[way][0])
                def _():
                    for copy in halo_copies(buffer, turn, c, way):
                        copy.wait_send()


def fused(pattern, send_list, owner_map, heat, active, diagonal, conductance, displacement, bonds, devices, ny):
    blocks, length, cases = heat.shape
    ghosts = send_list.shape[1] * send_list.shape[2]
    places = devices * max(1, blocks // devices)
    smem = pl.BlockSpec(memory_space=pltpu.SMEM)
    vmem = pl.BlockSpec(memory_space=pltpu.VMEM)
    hbm = pl.BlockSpec(memory_space=pl.ANY)
    state = pltpu.VMEM((blocks, length, cases), jnp.float32)
    ext = pltpu.VMEM((max(blocks + ghosts, (blocks // ny + 2) * (ny + 2)), length, cases), jnp.bfloat16)
    half = pltpu.VMEM((blocks, length, cases), jnp.bfloat16)
    dma = pltpu.SemaphoreType.DMA
    result = pltpu.VMEM((blocks, length, cases), jnp.bfloat16)
    return pl.pallas_call(
        functools.partial(fused_kernel, ny),
        out_shape=(result, result),
        in_specs=[smem, smem, vmem, hbm, vmem, vmem, hbm, hbm, vmem],
        out_specs=(vmem, vmem),
        scratch_shapes=[
            pltpu.VMEM(conductance.shape, jnp.bfloat16),
            ext,
            ext,
            ext,
            pltpu.VMEM((ghosts + max(ghosts, places), length, cases), jnp.bfloat16),
            state,
            state,
            state,
            half,
            state,
            pltpu.VMEM((8, LANES), jnp.int32),
            pltpu.SMEM((8, LANES), jnp.int32),
            *[
                pltpu.VMEM((places, length // sum(Z_SHARES) * share, cases), jnp.bfloat16)
                for share in Z_SHARES
            ],
            dma,
            dma,
            dma,
            dma((ITERS, len(GHOST_STEPS), PIECES)),
            dma((ITERS, len(GHOST_STEPS), PIECES)),
            dma((Z_CHUNKS, devices)),
            dma((Z_CHUNKS, devices)),
            dma((2, Z_CHUNKS, 2, 2)),
            dma((2, Z_CHUNKS, 2, ny, 2)),
        ],
        compiler_params=pltpu.CompilerParams(
            collective_id=0, has_side_effects=True, vmem_limit_bytes=57 * MIB
        ),
        name="fused",
    )(pattern, send_list, owner_map, heat, active, diagonal, conductance, displacement, bonds)


def settle_kernel(bricks, moved, bricks_out, moved_out, sems):
    copies = []
    for i, (source, target) in enumerate(((bricks, bricks_out), (moved, moved_out))):
        half = source.shape[0] // 2
        for j in range(2):
            part = pl.ds(j * half, half)
            copies.append(
                pltpu.make_async_copy(source.at[part], target.at[part], sems.at[i, j])
            )
    for copy in copies:
        copy.start()
    for copy in copies:
        copy.wait()


def settle(bricks, moved):
    vmem = pl.BlockSpec(memory_space=pltpu.VMEM)
    hbm = pl.BlockSpec(memory_space=pl.ANY)
    result = jax.ShapeDtypeStruct(bricks.shape, bricks.dtype)
    return pl.pallas_call(
        settle_kernel,
        out_shape=(result, result),
        in_specs=[vmem, vmem],
        out_specs=(hbm, hbm),
        scratch_shapes=[pltpu.SemaphoreType.DMA((2, 2))],
        compiler_params=pltpu.CompilerParams(vmem_limit_bytes=8 * MIB),
        name="settle",
    )(bricks, moved)


def local(
    heat_source,
    diagonal,
    active,
    conductance,
    pattern,
    send_list,
    owner_map,
    displacement,
    bond_live,
):
    blocks, tile_count, length = conductance.shape[:3]
    cases = heat_source.shape[1]
    devices = lax.axis_size(("row", "col"))

    bricks, moved = fused(
        pattern.T,
        send_list,
        owner_map,
        heat_source.reshape(blocks, length, cases),
        active.reshape(blocks, length),
        diagonal.reshape(blocks, length),
        conductance,
        displacement.reshape(blocks, length, cases),
        bond_live.reshape(-1, length),
        devices,
        displacement.shape[1],
    )
    bricks, moved = settle(
        bricks,
        moved,
    )
    return (bricks.reshape(displacement.shape), moved.reshape(displacement.shape))


def solution(mesh):
    return jax.shard_map(
        local,
        mesh=mesh,
        in_specs=(
            P(("row", "col"), None),
            P(("row", "col")),
            P(("row", "col")),
            P(("row", "col"), None, None, None),
            P(("row", "col"), None),
            P(("row", "col"), None, None),
            P(),
            P("row", "col", None, None),
            P(None, "row", "col", None),
        ),
        out_specs=(P("row", "col", None, None), P("row", "col", None, None)),
        check_vma=False,
    )
```
